256 devices in a mesh: groups: 128 (over z, y, x), mp: 2 (over core).
Axes of the slice: x: 4, y: 4, z: 8, core: 2. Of those that a mesh axis runs over, the one named last changes fastest.
Arguments:
- latents: float32 [12288, 256], P('groups', 'mp'), may hold values from -6 to 6
- tile_slot: int32 [12288], replicated, may hold values from 0 to 12287, as said below
- live: int32 [128], replicated, may hold values from 192 to 384, as said below
- partner: int32 [128], replicated, may hold values from 0 to 127, as said below
- text_states: bfloat16 [128, 2, 154, 2432], P('groups'), may hold values from -6 to 6
- modulation: float32 [128, 2, 5, 2432], P('groups'), may hold values from -3 to 3
- w_embed: bfloat16 [64, 2432], replicated, may hold values from -0.75 to 0.75
- w_qkv: bfloat16 [2432, 3, 1280], P(None, None, 'mp'), may hold values from -0.125 to 0.125
- w_text_kv: bfloat16 [2432, 2, 1280], P(None, None, 'mp'), may hold values from -0.125 to 0.125
- w_out: bfloat16 [1280, 2432], P('mp'), may hold values from -0.15625 to 0.15625
- w_final: bfloat16 [2432, 64], replicated, may hold values from -0.125 to 0.125
- norm_gains: float32 [3, 64], replicated, may hold values from 0.5 to 24
Outputs:
- new_latents: float32 [12288, 256], P('groups', 'mp')
The draws below stay inside these ranges and needn't reach their ends.
Inputs may be any that keep to these rules, and one draw needn't show every extreme that they name: `tile_slot`: every slot appears once; the tiles of one group go to any one group at most 2 times, and exactly 2 times for some pairs of groups. `live`: two groups that share a request hold equal counts; some group is full in every draw. partner[g] is g or g with its lowest bit flipped, and partner[partner[g]] = g; some pair shares a request in every draw.
All inputs are finite; a program needn't handle non-finite values.
Results may differ from the reference program's by a relative error of at most 0.012.
The reference program's roundings to bfloat16 on the way (of `normed`, `query`, `weights`, `attended` and `final`) count: a program that leaves them out, or rounds other values in their place, can miss the bound.
Values may be sent and summed in bfloat16 or wider, within the bound.
A program may use at most 128 MiB of HBM per device.

```python
import math
import jax
import jax.numpy as jnp
from jax import lax

D = 2432
HEADS = 20
HEAD = 64
CH = 64
TEXT = 154
ROWS = 384
TILE = 4
GROUPS = 128
TILES = 96
CAP = 2
N_GROUPS = 128
N_MP = 2


def draw_tile_slot(key, part):
    first_key, second_key = jax.random.split(jax.random.fold_in(key, 11))
    mixed_shifts = jax.random.permutation(first_key, GROUPS).astype(jnp.int32)
    places = jnp.arange(GROUPS, dtype=jnp.int32)
    priority = jnp.where(mixed_shifts == 1, -3, jnp.where(mixed_shifts == GROUPS - 1, -2, jnp.where(mixed_shifts == GROUPS // 2, -1, places)))
    ordered = mixed_shifts[jnp.argsort(priority, stable=True)]
    shifts = ordered[:TILES // CAP]
    tile_ids = jnp.arange(TILES, dtype=jnp.int32)
    owners = jnp.arange(GROUPS, dtype=jnp.int32)
    target = (owners[:, None] + shifts[tile_ids // CAP][None, :]) % GROUPS
    orders = jax.vmap(lambda one_key: jax.random.permutation(one_key, TILES))(jax.random.split(second_key, GROUPS))
    placed = orders[target, jnp.broadcast_to(tile_ids[None, :], target.shape)]
    return (target * TILES + placed).reshape(-1).astype(jnp.int32)


def pair_tables(key):
    first_key, second_key, third_key, fourth_key = jax.random.split(jax.random.fold_in(key, 7), 4)
    half_groups = GROUPS // 2
    joined = jax.random.randint(first_key, (half_groups,), 0, 2)
    forced = jax.random.randint(second_key, (), 0, half_groups)
    joined = joined.at[forced].set(1)
    lengths = jax.random.randint(third_key, (GROUPS,), ROWS // 2, ROWS + 1)
    shared = jax.random.randint(fourth_key, (half_groups,), ROWS // 2, ROWS + 1)
    shared = shared.at[forced].set(ROWS)
    joined_rows = jnp.repeat(joined, 2)
    lengths = jnp.where(joined_rows == 1, jnp.repeat(shared, 2), lengths)
    group_ids = jnp.arange(GROUPS, dtype=jnp.int32)
    mates = jnp.where(joined_rows == 1, jnp.bitwise_xor(group_ids, 1), group_ids)
    return (lengths.astype(jnp.int32), mates.astype(jnp.int32))


def draw_live(key, part):
    return pair_tables(key)[0]


def draw_partner(key, part):
    return pair_tables(key)[1]


def draw_norm_gains(key, part):
    first_key = jax.random.fold_in(jax.random.fold_in(key, 3), 0)
    lower = jnp.exp(jax.random.uniform(first_key, (3, HEAD), jnp.float32, math.log(0.5), math.log(2.0)))
    return lower


def block_levels(rng, dims, pieces, low, largest):
    factor_of = 1.0
    for dim, shards_of in pieces:
        draws = jax.random.uniform(jax.random.fold_in(jax.random.fold_in(rng, 6), dim), (shards_of,), jnp.float32, low / len(pieces), largest / len(pieces))
        factor_of = factor_of * jnp.repeat(jnp.exp(draws), dims[dim] // shards_of).reshape((-1,) + (1,) * (len(dims) - 1 - dim))
    return factor_of


def gaussian(key, dims, scale, limit, shards=(), held_as=jnp.bfloat16):
    entries = jax.random.normal(key, dims, jnp.float32) * scale
    if len(shards) > 0:
        entries = block_levels(key, dims, shards, -0.22, 0.18) * entries
    return jnp.clip(entries, min=-limit, max=limit).astype(held_as)


def setup_inputs(seed: int = 0) -> dict:
    arg_keys = jax.random.split(jax.random.key(seed), 13)
    latents = gaussian(arg_keys[0], (GROUPS * TILES, TILE * CH), 1.0, 6.0, ((0, 128), (1, 2)), jnp.float32)
    tile_slot = draw_tile_slot(jax.random.fold_in(arg_keys[12], 71), 0)
    live = draw_live(jax.random.fold_in(arg_keys[12], 71), 0)
    partner = draw_partner(jax.random.fold_in(arg_keys[12], 71), 0)
    text_states = gaussian(arg_keys[4], (GROUPS, 2, TEXT, D), 1.0, 6.0, ((0, 128),))
    modulation = gaussian(arg_keys[5], (GROUPS, 2, 5, D), 0.5, 3.0, ((0, 128),), jnp.float32)
    w_embed = gaussian(arg_keys[6], (CH, D), CH ** -0.5, 0.75)
    w_qkv = gaussian(arg_keys[7], (D, 3, HEADS * HEAD), D ** -0.5, 0.125, ((2, 2),))
    w_text_kv = gaussian(arg_keys[8], (D, 2, HEADS * HEAD), D ** -0.5, 0.125, ((2, 2),))
    w_out = gaussian(arg_keys[9], (HEADS * HEAD, D), (HEADS * HEAD) ** -0.5, 0.15625, ((0, 2),))
    w_final = gaussian(arg_keys[10], (D, CH), D ** -0.5, 0.125)
    norm_gains = draw_norm_gains(jax.random.fold_in(arg_keys[12], 71), 0)
    return dict(latents=latents, tile_slot=tile_slot, live=live, partner=partner, text_states=text_states, modulation=modulation, w_embed=w_embed, w_qkv=w_qkv, w_text_kv=w_text_kv, w_out=w_out, w_final=w_final, norm_gains=norm_gains)


GUIDE = 3.5
STEP = -0.25
EPS = 1e-06

def layer_norm(inputs):
    centre = lax.optimization_barrier(jnp.mean(inputs, axis=-1, keepdims=True))
    centred = inputs - centre
    spread = lax.optimization_barrier(jnp.mean(centred * centred, axis=-1, keepdims=True))
    return centred * lax.rsqrt(spread + EPS)

def head_norm(inputs, gains):
    square = lax.optimization_barrier(jnp.mean(inputs * inputs, axis=-1, keepdims=True))
    return (inputs * lax.rsqrt(square + EPS) * gains).astype(jnp.bfloat16)

def finish(residue, mixed, adaptive, w_final):
    state = residue + adaptive[:, 2, None, :] * mixed
    final = (layer_norm(state) * (1.0 + adaptive[:, 4, None, :]) + adaptive[:, 3, None, :]).astype(jnp.bfloat16)
    velocity = jnp.einsum('brd,dc->brc', final.astype(jnp.float32), w_final.astype(jnp.float32))
    return velocity[1] + GUIDE * (velocity[0] - velocity[1])

def reference(latents, tile_slot, live, partner, text_states, modulation, w_embed, w_qkv, w_text_kv, w_out, w_final, norm_gains):
    width = HEADS * HEAD
    buffer = jnp.zeros_like(latents).at[tile_slot].set(latents)
    tokens = buffer.reshape(N_GROUPS, ROWS, CH)
    qkv_weight = w_qkv.astype(jnp.float32)
    text_weight = w_text_kv.astype(jnp.float32)
    out_blocks = w_out.astype(jnp.float32).reshape(N_MP, width // N_MP, D)

    def embed(group_index):
        hidden = jnp.dot(tokens[group_index].astype(jnp.bfloat16), w_embed, preferred_element_type=jnp.float32)
        return hidden

    def project(group_index):
        hidden = embed(group_index)
        adaptive = modulation[group_index]
        normed = (layer_norm(hidden)[None] * (1.0 + adaptive[:, 1, None, :]) + adaptive[:, 0, None, :]).astype(jnp.bfloat16)
        projected = jnp.einsum('brd,dcn->brcn', normed.astype(jnp.float32), qkv_weight).reshape(2, ROWS, 3, HEADS, HEAD)
        query = head_norm(projected[:, :, 0], norm_gains[0])
        image_key = head_norm(projected[:, :, 1], norm_gains[1])
        image_value = projected[:, :, 2].astype(jnp.bfloat16)
        return (query, image_key, image_value)
    queries, image_keys, image_values = lax.map(project, jnp.arange(N_GROUPS, dtype=jnp.int32))
    position = jnp.arange(ROWS, dtype=jnp.int32)

    def attend(group_index):
        mate = partner[group_index]
        joined = mate != group_index
        own_len = live[group_index]
        mate_len = jnp.where(joined, live[mate], 0)
        text_proj = jnp.einsum('btd,dcn->btcn', text_states[group_index].astype(jnp.float32), text_weight).reshape(2, TEXT, 2, HEADS, HEAD)
        text_key = head_norm(text_proj[:, :, 0], norm_gains[2])
        text_value = text_proj[:, :, 1].astype(jnp.bfloat16)
        all_keys = jnp.concatenate([text_key, image_keys[group_index], image_keys[mate]], axis=1)
        all_values = jnp.concatenate([text_value, image_values[group_index], image_values[mate]], axis=1)
        usable = jnp.concatenate([jnp.ones((TEXT,), bool), position < own_len, position < mate_len])
        scores = jnp.einsum('bqhe,bkhe->bhqk', queries[group_index].astype(jnp.float32), all_keys.astype(jnp.float32)) * HEAD ** (-0.5)
        scores = jnp.where(usable[None, None, None, :], scores, -1e+30)
        highest = lax.optimization_barrier(jnp.max(scores, axis=-1, keepdims=True))
        raised = jnp.exp(scores - highest)
        summed = lax.optimization_barrier(jnp.sum(raised, axis=-1, keepdims=True))
        weights = (raised / summed).astype(jnp.bfloat16)
        attended = jnp.einsum('bhqk,bkhe->bqhe', weights.astype(jnp.float32), all_values.astype(jnp.float32)).astype(jnp.bfloat16)
        blocks = attended.reshape(2, ROWS, N_MP, width // N_MP).astype(jnp.float32)
        terms = jnp.einsum('brmn,mnd->mbrd', blocks, out_blocks).astype(jnp.bfloat16)
        terms = lax.optimization_barrier(terms).astype(jnp.float32)
        mixed = lax.optimization_barrier(jnp.sum(terms, axis=0))
        hidden = embed(group_index)
        guided = finish(hidden[None], mixed, modulation[group_index], w_final)
        living = (position < own_len)[:, None]
        return tokens[group_index] + STEP * jnp.where(living, guided, 0.0)
    updated = lax.map(attend, jnp.arange(N_GROUPS, dtype=jnp.int32))
    new_buffer = updated.reshape(N_GROUPS * TILES, TILE * CH)
    return new_buffer[tile_slot]
```

```python
import functools
import jax
import jax.numpy as jnp
from jax import lax
from jax.experimental import pallas as pl
from jax.experimental.pallas import tpu as pltpu
from jax.sharding import PartitionSpec as P

HEAD = 64
CH = 64
TEXT = 154
ROWS = 384
TILE = 4
TILES = 96
D = 2432
Z = 8
XY = 16
HALF = ROWS // 2

GUIDE = 3.5
STEP = -0.25
EPS = 1e-06
F32 = jnp.float32
BF16 = jnp.bfloat16
MESH = pl.DeviceIdType.MESH
VMEM = pl.BlockSpec(memory_space=pltpu.VMEM)
SMEM = pl.BlockSpec(memory_space=pltpu.SMEM)


def iota(shape, axis):
    return lax.broadcasted_iota(jnp.int32, shape, axis)


def onehot(condition):
    return jnp.where(condition, 1.0, 0.0).astype(BF16)


def group_of(slot):
    return (slot * 43691) >> 22


def where_am_i():
    group = lax.axis_index("groups")
    return group, lax.axis_index("mp"), lax.div(group, XY), lax.rem(group, XY)


def z_peer(z, k):
    return lax.rem(z + k, Z)


def my_buckets_row(slot_ref, group):
    mine = jnp.broadcast_to(group_of(slot_ref[pl.ds(group, 1), :]).astype(F32), (TILES, TILES))
    across, down = iota((TILES, TILES), 1), iota((TILES, TILES), 0)
    column = jnp.sum(jnp.where(across == down, mine, 0.0), axis=1, keepdims=True)
    earlier = jnp.where((mine == column) & (down < across), 1.0, 0.0)
    return 2.0 * mine[:1] + jnp.sum(earlier, axis=0, keepdims=True)


def my_buckets_column(slot_ref, group):
    mine = jnp.broadcast_to(group_of(slot_ref[pl.ds(group, 1), :]).astype(F32), (TILES, TILES))
    across, down = iota((TILES, TILES), 1), iota((TILES, TILES), 0)
    column = jnp.sum(jnp.where(across == down, mine, 0.0), axis=1, keepdims=True)
    earlier = jnp.where((mine == column) & (across < down), 1.0, 0.0)
    return 2.0 * column + jnp.sum(earlier, axis=1, keepdims=True)


def landing(slot_ref, rows, source, wanted, rank_wanted):
    slot = slot_ref[...]
    target = group_of(slot)
    placed = slot - target * TILES
    pick = onehot(iota((rows, Z * XY), 1) == source)
    goal = jnp.dot(pick, target.astype(F32).astype(BF16), preferred_element_type=F32)
    place = jnp.dot(pick, placed.astype(F32).astype(BF16), preferred_element_type=F32)
    matched = jnp.where(goal == wanted, 1.0, 0.0)
    before = onehot(iota((TILES, TILES), 0) < iota((TILES, TILES), 1))
    rank = jnp.dot(matched.astype(BF16), before, preferred_element_type=F32)
    return jnp.where((matched > 0.5) & (rank == rank_wanted), place + 1.0, 0.0)


def deal_kernel(
    lat_ref, slot_ref, mod_ref, own_ref, par_ref, modp_ref,
    buf_s, buf_a, buf_b, buf_c, mod_s, ssem_a, rsem_a, ssem_b, rsem_b, msem,
):
    group, core, z, xy = where_am_i()
    me = xy * 2 + core
    mate = group + 1 - 2 * lax.rem(group, 2)
    barrier = pltpu.get_barrier_semaphore()

    def z_id(k):
        return {"groups": z_peer(z, k) * XY + xy, "mp": core}

    def plane(k):
        t = lax.rem(me + k, 2 * XY)
        return lax.div(t, 2), lax.rem(t, 2)

    def plane_id(k):
        at, other = plane(k)
        return {"groups": z * XY + at, "mp": other}

    @pl.loop(1, Z)
    def _(k):
        pl.semaphore_signal(barrier, inc=1, device_id=z_id(k), device_id_type=MESH)

    @pl.loop(1, 2 * XY)
    def _(k):
        pl.semaphore_signal(barrier, inc=1, device_id=plane_id(k), device_id_type=MESH)

    sender = onehot(iota((256, TILES), 0).astype(F32) == my_buckets_row(slot_ref, group))
    buf_s[...] = (
        jnp.dot(sender, lat_ref[...].astype(BF16), preferred_element_type=F32)
        .astype(BF16).reshape(Z, 32, 128)
    )
    pl.semaphore_wait(barrier, Z - 1 + 2 * XY - 1)

    def send_a(k):
        return pltpu.make_async_remote_copy(
            src_ref=buf_s.at[z_peer(z, k)], dst_ref=buf_a.at[z],
            send_sem=ssem_a.at[k], recv_sem=rsem_a.at[z],
            device_id=z_id(k), device_id_type=MESH,
        )

    def come_a(k):
        other = z_peer(z, k)
        return pltpu.make_async_remote_copy(
            src_ref=buf_s.at[other], dst_ref=buf_a.at[other],
            send_sem=ssem_a.at[k], recv_sem=rsem_a.at[other],
            device_id=z_id(k), device_id_type=MESH,
        )

    @pl.loop(1, Z)
    def _(k):
        send_a(k).start()

    mod_copy = pltpu.make_async_remote_copy(
        src_ref=mod_ref.at[pl.ds(0, 2)], dst_ref=mod_s,
        send_sem=msem.at[0], recv_sem=msem.at[1],
        device_id={"groups": mate, "mp": core}, device_id_type=MESH,
    )
    mod_copy.start()
    buf_a[z] = buf_s[z]

    row = iota((512, 1), 0)
    low = group - lax.rem(group, 2)
    brought = landing(
        slot_ref, 512, (row & 7) * XY + (row >> 5),
        (low + ((row >> 4) & 1)).astype(F32), ((row >> 3) & 1).astype(F32),
    )
    spot = lax.dot_general(
        jnp.ones((8, TILES), BF16), brought.astype(BF16), (((1,), (1,)), ((), ())),
        preferred_element_type=F32,
    )[:1]
    hit = iota((TILES, 512), 0).astype(F32) + 1.0 == spot
    member = (iota((TILES, 512), 1) >> 4) & 1
    bit = lax.rem(group, 2)
    take_own = onehot(hit & (member == bit))
    take_par = onehot(hit & (member != bit))
    out_row = iota((256, 256), 0)
    reorder = onehot(
        iota((256, 256), 1) == (out_row & 7) * 32 + (out_row >> 4) * 2 + ((out_row >> 3) & 1)
    )

    @pl.loop(1, Z)
    def _(k):
        come_a(k).wait_recv()

    buf_b[...] = (
        jnp.dot(reorder, buf_a[...].reshape(256, 128), preferred_element_type=F32)
        .astype(BF16).reshape(Z, 32, 128)
    )

    def send_b(k):
        at, other = plane(k)
        return pltpu.make_async_remote_copy(
            src_ref=buf_b.at[lax.div(at, 2)], dst_ref=buf_c.at[core, xy],
            send_sem=ssem_b.at[k], recv_sem=rsem_b.at[me],
            device_id=plane_id(k), device_id_type=MESH,
        )

    def come_b(k):
        at, other = plane(k)
        return pltpu.make_async_remote_copy(
            src_ref=buf_b.at[lax.div(at, 2)], dst_ref=buf_c.at[other, at],
            send_sem=ssem_b.at[k], recv_sem=rsem_b.at[at * 2 + other],
            device_id=plane_id(k), device_id_type=MESH,
        )

    @pl.loop(1, 2 * XY)
    def _(k):
        send_b(k).start()

    buf_c[core, xy] = buf_b[lax.div(xy, 2)]

    @pl.loop(1, 2 * XY)
    def _(k):
        come_b(k).wait_recv()

    for half in range(2):
        landed = buf_c[half].reshape(512, 128)
        for take, out in ((take_own, own_ref), (take_par, par_ref)):
            tiles = jnp.dot(take, landed, preferred_element_type=F32).astype(BF16)
            out[2 * half] = tiles[:, :CH]
            out[2 * half + 1] = tiles[:, CH:]

    mod_copy.wait_recv()
    modp_ref[...] = mod_s[...]

    @pl.loop(1, Z)
    def _(k):
        send_a(k).wait_send()

    @pl.loop(1, 2 * XY)
    def _(k):
        send_b(k).wait_send()

    mod_copy.wait_send()


def deal(latents, slots, mod):
    return pl.pallas_call(
        deal_kernel,
        out_shape=(
            jax.ShapeDtypeStruct((TILE, TILES, CH), BF16),
            jax.ShapeDtypeStruct((TILE, TILES, CH), BF16),
            jax.ShapeDtypeStruct((2, 2, D), F32),
        ),
        in_specs=[VMEM] * 3,
        out_specs=(VMEM,) * 3,
        scratch_shapes=[
            pltpu.VMEM((Z, 32, 128), BF16),
            pltpu.VMEM((Z, 32, 128), BF16),
            pltpu.VMEM((Z, 32, 128), BF16),
            pltpu.VMEM((2, XY, 32, 128), BF16),
            pltpu.VMEM((2, 2, D), F32),
            pltpu.SemaphoreType.DMA((Z,)),
            pltpu.SemaphoreType.DMA((Z,)),
            pltpu.SemaphoreType.DMA((2 * XY,)),
            pltpu.SemaphoreType.DMA((2 * XY,)),
            pltpu.SemaphoreType.DMA((2,)),
        ],
        compiler_params=pltpu.CompilerParams(collective_id=0, has_side_effects=True),
        name="deal",
    )(latents, slots, mod)


CHUNKS = ((0, 512), (512, 512), (1024, 512), (1536, 512), (2048, 384))


def home_kernel(
    att_ref, wout_ref, tok_ref, wemb_ref, wfin_ref, mod_ref, live_ref, lat_ref, slot_ref, out_ref,
    give, got, kept, hid, vel, buf_d, buf_e, buf_f, buf_g, xsend, xrecv, ssem_b, rsem_b, ssem_a, rsem_a,
):
    group, core, z, xy = where_am_i()
    other = 1 - core
    barrier = pltpu.get_barrier_semaphore()

    def z_id(k):
        return {"groups": z_peer(z, k) * XY + xy, "mp": core}

    def plane(k):
        return lax.rem(xy + k, XY)

    def plane_id(k):
        return {"groups": z * XY + plane(k), "mp": core}

    sibling = {"groups": group, "mp": other}
    pl.semaphore_signal(barrier, inc=1, device_id=sibling, device_id_type=MESH)

    @pl.loop(1, Z)
    def _(k):
        pl.semaphore_signal(barrier, inc=1, device_id=z_id(k), device_id_type=MESH)

    @pl.loop(1, XY)
    def _(k):
        pl.semaphore_signal(barrier, inc=1, device_id=plane_id(k), device_id_type=MESH)

    def exchange(b):
        return pltpu.make_async_remote_copy(
            src_ref=give.at[b], dst_ref=got.at[b], send_sem=xsend.at[b], recv_sem=xrecv.at[b],
            device_id=sibling, device_id_type=MESH,
        )

    def project(b, half, dst):
        rows = att_ref[b, half]
        for start, size in CHUNKS:
            dst[b, :, start:start + size] = jnp.dot(
                rows, wout_ref[:, start:start + size], preferred_element_type=F32
            ).astype(BF16)

    for b in range(2):
        project(b, other, give)
        if b == 0:
            pl.semaphore_wait(barrier, 1 + Z - 1 + XY - 1)
        exchange(b).start()
    for b in range(2):
        project(b, core, kept)
    for start, size in CHUNKS:
        hid[:, start:start + size] = jnp.dot(
            tok_ref[core], wemb_ref[:, start:start + size], preferred_element_type=F32
        )

    block = 48
    for b in range(2):
        exchange(b).wait_recv()
        gate, shift, scale = (mod_ref[i, b:b + 1, :] for i in (2, 3, 4))

        @pl.loop(0, HALF // block)
        def _(i):
            rows = pl.ds(pl.multiple_of(i * block, block), block)
            mixed = kept[b, rows, :].astype(F32) + got[b, rows, :].astype(F32)
            state = hid[rows, :] + gate * mixed
            centred = state - jnp.mean(state, axis=-1, keepdims=True)
            spread = jnp.mean(centred * centred, axis=-1, keepdims=True)
            final = (centred * lax.rsqrt(spread + EPS) * (1.0 + scale) + shift).astype(BF16)
            vel[b, rows, :] = lax.dot_general(
                final, wfin_ref[...], (((1,), (1,)), ((), ())), preferred_element_type=F32
            )

    guided = vel[1] + GUIDE * (vel[0] - vel[1])
    row = iota((HALF, CH), 0)
    upper = jnp.where(row >= TILES, 1, 0)
    position = (row - upper * TILES) * TILE + 2 * core + upper
    change = jnp.where(position < live_ref[group], STEP * guided, 0.0)
    change = jnp.concatenate([change[:TILES], change[TILES:]], axis=1).astype(BF16)

    row = iota((256, 1), 0)
    brought = landing(
        slot_ref, 256, (row & 7) * XY + (row >> 4), group.astype(F32), ((row >> 3) & 1).astype(F32)
    )
    spot = jnp.sum(brought, axis=1, keepdims=True)
    back = onehot(spot == iota((256, TILES), 1).astype(F32) + 1.0)
    buf_d[...] = (
        jnp.dot(back, change, preferred_element_type=F32).astype(BF16).reshape(XY, 16, 128)
    )

    def send_b(k):
        return pltpu.make_async_remote_copy(
            src_ref=buf_d.at[plane(k)], dst_ref=buf_e.at[xy],
            send_sem=ssem_b.at[k], recv_sem=rsem_b.at[xy],
            device_id=plane_id(k), device_id_type=MESH,
        )

    def come_b(k):
        return pltpu.make_async_remote_copy(
            src_ref=buf_d.at[plane(k)], dst_ref=buf_e.at[plane(k)],
            send_sem=ssem_b.at[k], recv_sem=rsem_b.at[plane(k)],
            device_id=plane_id(k), device_id_type=MESH,
        )

    @pl.loop(1, XY)
    def _(k):
        send_b(k).start()

    buf_e[xy] = buf_d[xy]
    out_row = iota((256, 256), 0)
    reorder = onehot(
        iota((256, 256), 1) == ((out_row >> 1) & 15) * 16 + (out_row & 1) * 8 + (out_row >> 5)
    )
    gather = onehot(iota((TILES, 256), 1).astype(F32) == my_buckets_column(slot_ref, group))

    @pl.loop(1, XY)
    def _(k):
        come_b(k).wait_recv()

    buf_f[...] = (
        jnp.dot(reorder, buf_e[...].reshape(256, 128), preferred_element_type=F32)
        .astype(BF16).reshape(Z, 32, 128)
    )

    def send_a(k):
        return pltpu.make_async_remote_copy(
            src_ref=buf_f.at[z_peer(z, k)], dst_ref=buf_g.at[z],
            send_sem=ssem_a.at[k], recv_sem=rsem_a.at[z],
            device_id=z_id(k), device_id_type=MESH,
        )

    def come_a(k):
        return pltpu.make_async_remote_copy(
            src_ref=buf_f.at[z_peer(z, k)], dst_ref=buf_g.at[z_peer(z, k)],
            send_sem=ssem_a.at[k], recv_sem=rsem_a.at[z_peer(z, k)],
            device_id=z_id(k), device_id_type=MESH,
        )

    @pl.loop(1, Z)
    def _(k):
        send_a(k).start()

    buf_g[z] = buf_f[z]

    @pl.loop(1, Z)
    def _(k):
        come_a(k).wait_recv()

    out_ref[...] = lat_ref[...] + jnp.dot(
        gather, buf_g[...].reshape(256, 128), preferred_element_type=F32
    )

    for b in range(2):
        exchange(b).wait_send()

    @pl.loop(1, XY)
    def _(k):
        send_b(k).wait_send()

    @pl.loop(1, Z)
    def _(k):
        send_a(k).wait_send()


def home(attended, w_out, tokens, w_embed, w_final, mod, live, latents, slots):
    return pl.pallas_call(
        home_kernel,
        out_shape=jax.ShapeDtypeStruct((TILES, 128), F32),
        in_specs=[VMEM] * 6 + [SMEM] + [VMEM] * 2,
        out_specs=VMEM,
        scratch_shapes=[
            pltpu.VMEM((2, HALF, D), BF16),
            pltpu.VMEM((2, HALF, D), BF16),
            pltpu.VMEM((2, HALF, D), BF16),
            pltpu.VMEM((HALF, D), F32),
            pltpu.VMEM((2, HALF, CH), F32),
            pltpu.VMEM((XY, 16, 128), BF16),
            pltpu.VMEM((XY, 16, 128), BF16),
            pltpu.VMEM((Z, 32, 128), BF16),
            pltpu.VMEM((Z, 32, 128), BF16),
            pltpu.SemaphoreType.DMA((2,)),
            pltpu.SemaphoreType.DMA((2,)),
            pltpu.SemaphoreType.DMA((XY,)),
            pltpu.SemaphoreType.DMA((XY,)),
            pltpu.SemaphoreType.DMA((Z,)),
            pltpu.SemaphoreType.DMA((Z,)),
        ],
        compiler_params=pltpu.CompilerParams(
            collective_id=1, has_side_effects=True, vmem_limit_bytes=40 << 20
        ),
        name="home",
    )(attended, w_out, tokens, w_embed, w_final, mod, live, latents, slots)


def layer_norm(inputs):
    centre = jnp.mean(inputs, axis=-1, keepdims=True)
    centred = inputs - centre
    spread = jnp.mean(centred * centred, axis=-1, keepdims=True)
    return centred * lax.rsqrt(spread + EPS)


def head_norm(inputs, gains):
    square = jnp.mean(inputs * inputs, axis=-1, keepdims=True)
    return (inputs * lax.rsqrt(square + EPS) * gains).astype(BF16)


def shards(
    latents, tile_slot, live, partner, text_states, modulation,
    w_embed, w_qkv, w_text_kv, w_out, w_final, norm_gains,
):
    group = lax.axis_index("groups")
    slots = tile_slot.reshape(Z * XY, TILES)
    mod = modulation[0].transpose(1, 0, 2)
    own, par, mod_par = deal(latents, slots, mod)
    tokens = jnp.concatenate([own.reshape(ROWS, CH), par.reshape(ROWS, CH)], axis=0)
    hidden = jnp.dot(tokens, w_embed, preferred_element_type=F32)
    scaled = layer_norm(hidden).reshape(2, 1, ROWS, D)
    mods = jnp.stack([mod[:2], mod_par])
    normed = (scaled * (1.0 + mods[:, 1, :, None, :]) + mods[:, 0, :, None, :]).astype(BF16)
    w3 = w_qkv.transpose(1, 0, 2)
    local_heads = w_qkv.shape[2] // HEAD
    query = jnp.dot(normed[0].reshape(2 * ROWS, D), w3[0], preferred_element_type=F32)
    keys = jnp.dot(normed.reshape(4 * ROWS, D), w3[1], preferred_element_type=F32)
    values = jnp.dot(normed.reshape(4 * ROWS, D), w3[2], preferred_element_type=F32)
    query = head_norm(query.reshape(2, ROWS, local_heads, HEAD), norm_gains[0])
    keys = head_norm(keys.reshape(2, 2, ROWS, local_heads, HEAD), norm_gains[1])
    values = values.reshape(2, 2, ROWS, local_heads, HEAD).astype(BF16)
    text_proj = jnp.einsum("btd,dcn->btcn", text_states[0], w_text_kv, preferred_element_type=F32)
    text_proj = text_proj.reshape(2, TEXT, 2, local_heads, HEAD)
    text_key = head_norm(text_proj[:, :, 0], norm_gains[2])
    text_value = text_proj[:, :, 1].astype(BF16)
    mate = partner[group]
    own_len = live[group]
    mate_len = jnp.where(mate != group, live[mate], 0)
    order = jnp.arange(ROWS, dtype=jnp.int32)
    position = (order % TILES) * TILE + order // TILES
    all_keys = jnp.concatenate([text_key, keys[0], keys[1]], axis=1)
    all_values = jnp.concatenate([text_value, values[0], values[1]], axis=1)
    usable = jnp.concatenate([jnp.ones((TEXT,), bool), position < own_len, position < mate_len])

    def branch_attention(items):
        branch_query, branch_keys, branch_values = items
        scores = jnp.einsum(
            "qhe,khe->hqk", branch_query, branch_keys, preferred_element_type=F32
        ) * HEAD ** (-0.5)
        scores = jnp.where(usable[None, None, :], scores, -1e30)
        highest = jnp.max(scores, axis=-1, keepdims=True)
        raised = jnp.exp(scores - highest)
        summed = jnp.sum(raised, axis=-1, keepdims=True)
        weights = (raised / summed).astype(BF16)
        result_heads = jnp.einsum(
            "hqk,khe->qhe", weights, branch_values, preferred_element_type=F32
        )
        return result_heads.astype(BF16)

    attended = lax.map(branch_attention, (query, all_keys, all_values))
    return home(
        attended.reshape(2, 2, HALF, local_heads * HEAD), w_out, own.reshape(2, HALF, CH),
        w_embed, w_final.T, mod, live, latents, slots,
    )


def solution(mesh):
    placed = (
        P("groups", "mp"), P(), P(), P(),
        P("groups", None, None, None), P("groups", None, None, None),
        P(), P(None, None, "mp"), P(None, None, "mp"), P("mp", None), P(), P(),
    )
    return jax.shard_map(
        shards, mesh=mesh, in_specs=placed, out_specs=P("groups", "mp"), check_vma=False
    )
```

```python
import functools
import jax
import jax.numpy as jnp
from jax import lax
from jax.experimental import pallas as pl
from jax.experimental.pallas import tpu as pltpu
from jax.sharding import PartitionSpec as P

HEAD = 64
CH = 64
TEXT = 154
ROWS = 384
TILE = 4
TILES = 96
D = 2432
Z = 8
XY = 16
HALF = ROWS // 2
TEXT_PAD = 160
KEYS = 2 * ROWS + TEXT_PAD
WIDTH = 640
SLABS = WIDTH // 128

GUIDE = 3.5
STEP = -0.25
EPS = 1e-06
F32 = jnp.float32
BF16 = jnp.bfloat16
MESH = pl.DeviceIdType.MESH
VMEM = pl.BlockSpec(memory_space=pltpu.VMEM)
SMEM = pl.BlockSpec(memory_space=pltpu.SMEM)


def iota(shape, axis):
    return lax.broadcasted_iota(jnp.int32, shape, axis)


def onehot(condition):
    return jnp.where(condition, 1.0, 0.0).astype(BF16)


def group_of(slot):
    return (slot * 43691) >> 22


def where_am_i():
    group = lax.axis_index("groups")
    return group, lax.axis_index("mp"), lax.div(group, XY), lax.rem(group, XY)


def z_peer(z, k):
    return lax.rem(z + k, Z)


def my_buckets_row(slot_ref, group):
    mine = jnp.broadcast_to(group_of(slot_ref[pl.ds(group, 1), :]).astype(F32), (TILES, TILES))
    across, down = iota((TILES, TILES), 1), iota((TILES, TILES), 0)
    column = jnp.sum(jnp.where(across == down, mine, 0.0), axis=1, keepdims=True)
    earlier = jnp.where((mine == column) & (down < across), 1.0, 0.0)
    return 2.0 * mine[:1] + jnp.sum(earlier, axis=0, keepdims=True)


def my_buckets_column(slot_ref, group):
    mine = jnp.broadcast_to(group_of(slot_ref[pl.ds(group, 1), :]).astype(F32), (TILES, TILES))
    across, down = iota((TILES, TILES), 1), iota((TILES, TILES), 0)
    column = jnp.sum(jnp.where(across == down, mine, 0.0), axis=1, keepdims=True)
    earlier = jnp.where((mine == column) & (across < down), 1.0, 0.0)
    return 2.0 * column + jnp.sum(earlier, axis=1, keepdims=True)


def landing(slot_ref, rows, source, wanted, rank_wanted):
    slot = slot_ref[...]
    target = group_of(slot)
    placed = slot - target * TILES
    pick = onehot(iota((rows, Z * XY), 1) == source)
    goal = jnp.dot(pick, target.astype(F32).astype(BF16), preferred_element_type=F32)
    place = jnp.dot(pick, placed.astype(F32).astype(BF16), preferred_element_type=F32)
    matched = jnp.where(goal == wanted, 1.0, 0.0)
    before = onehot(iota((TILES, TILES), 0) < iota((TILES, TILES), 1))
    rank = jnp.dot(matched.astype(BF16), before, preferred_element_type=F32)
    return jnp.where((matched > 0.5) & (rank == rank_wanted), place + 1.0, 0.0)


def head_norm(slab, gains):
    square = slab * slab
    lower = iota(slab.shape, 1) < HEAD
    first = jnp.sum(jnp.where(lower, square, 0.0), axis=-1, keepdims=True) * (1.0 / HEAD)
    second = jnp.sum(jnp.where(lower, 0.0, square), axis=-1, keepdims=True) * (1.0 / HEAD)
    return slab * jnp.where(lower, lax.rsqrt(first + EPS), lax.rsqrt(second + EPS)) * gains


def deal_kernel(
    lat_ref, slot_ref, mod_ref, gain_ref, text_hbm, wtext_hbm,
    tok_ref, modp_ref, tk_ref, tv_ref,
    buf_s, buf_a, buf_b, buf_c, mod_s, text_pairs, text, w_pairs, w_split,
    ssem_a, rsem_a, ssem_b, rsem_b, msem, tsem,
):
    group, core, z, xy = where_am_i()
    me = xy * 2 + core
    mate = group + 1 - 2 * lax.rem(group, 2)
    barrier = pltpu.get_barrier_semaphore()

    def z_id(k):
        return {"groups": z_peer(z, k) * XY + xy, "mp": core}

    def plane(k):
        t = lax.rem(me + k, 2 * XY)
        return lax.div(t, 2), lax.rem(t, 2)

    def plane_id(k):
        at, other = plane(k)
        return {"groups": z * XY + at, "mp": other}

    @pl.loop(1, Z)
    def _(k):
        pl.semaphore_signal(barrier, inc=1, device_id=z_id(k), device_id_type=MESH)

    @pl.loop(1, 2 * XY)
    def _(k):
        pl.semaphore_signal(barrier, inc=1, device_id=plane_id(k), device_id_type=MESH)

    text_copy = pltpu.make_async_copy(text_hbm, text_pairs.at[pl.ds(0, TEXT)], tsem.at[0])
    w_copy = pltpu.make_async_copy(wtext_hbm, w_pairs, tsem.at[1])
    w_copy.start()
    text_copy.start()
    text_pairs[TEXT:] = jnp.zeros((TEXT_PAD - TEXT, 2, D), BF16)
    sender = onehot(iota((256, TILES), 0).astype(F32) == my_buckets_row(slot_ref, group))
    buf_s[...] = (
        jnp.dot(sender, lat_ref[...].astype(BF16), preferred_element_type=F32)
        .astype(BF16).reshape(Z, 32, 128)
    )
    pl.semaphore_wait(barrier, Z - 1 + 2 * XY - 1)

    def send_a(k):
        return pltpu.make_async_remote_copy(
            src_ref=buf_s.at[z_peer(z, k)], dst_ref=buf_a.at[z],
            send_sem=ssem_a.at[k], recv_sem=rsem_a.at[z],
            device_id=z_id(k), device_id_type=MESH,
        )

    def come_a(k):
        other = z_peer(z, k)
        return pltpu.make_async_remote_copy(
            src_ref=buf_s.at[other], dst_ref=buf_a.at[other],
            send_sem=ssem_a.at[k], recv_sem=rsem_a.at[other],
            device_id=z_id(k), device_id_type=MESH,
        )

    @pl.loop(1, Z)
    def _(k):
        send_a(k).start()

    mod_copy = pltpu.make_async_remote_copy(
        src_ref=mod_ref.at[pl.ds(0, 2)], dst_ref=mod_s,
        send_sem=msem.at[0], recv_sem=msem.at[1],
        device_id={"groups": mate, "mp": core}, device_id_type=MESH,
    )
    mod_copy.start()
    buf_a[z] = buf_s[z]

    part_row = iota((256, 256), 0)
    part = onehot(iota((256, 256), 1) == (part_row & 127) * 2 + (part_row >> 7))
    w_copy.wait()

    @pl.loop(0, D // 128)
    def _(i):
        rows = pl.ds(pl.multiple_of(i * 128, 128), 128)
        both = jnp.dot(part, w_pairs[rows].reshape(256, WIDTH), preferred_element_type=F32)
        w_split[0, rows, :] = both[:128].astype(BF16)
        w_split[1, rows, :] = both[128:].astype(BF16)

    row = iota((512, 1), 0)
    low = group - lax.rem(group, 2)
    brought = landing(
        slot_ref, 512, (row & 7) * XY + (row >> 5),
        (low + ((row >> 4) & 1)).astype(F32), ((row >> 3) & 1).astype(F32),
    )
    spot = lax.dot_general(
        jnp.ones((8, TILES), BF16), brought.astype(BF16), (((1,), (1,)), ((), ())),
        preferred_element_type=F32,
    )[:1]
    hit = iota((TILES, 512), 0).astype(F32) + 1.0 == spot
    member = (iota((TILES, 512), 1) >> 4) & 1
    bit = lax.rem(group, 2)
    take_own = onehot(hit & (member == bit))
    take_par = onehot(hit & (member != bit))
    out_row = iota((256, 256), 0)
    reorder = onehot(
        iota((256, 256), 1) == (out_row & 7) * 32 + (out_row >> 4) * 2 + ((out_row >> 3) & 1)
    )

    @pl.loop(1, Z)
    def _(k):
        come_a(k).wait_recv()

    buf_b[...] = (
        jnp.dot(reorder, buf_a[...].reshape(256, 128), preferred_element_type=F32)
        .astype(BF16).reshape(Z, 32, 128)
    )

    def send_b(k):
        at, other = plane(k)
        return pltpu.make_async_remote_copy(
            src_ref=buf_b.at[lax.div(at, 2)], dst_ref=buf_c.at[core, xy],
            send_sem=ssem_b.at[k], recv_sem=rsem_b.at[me],
            device_id=plane_id(k), device_id_type=MESH,
        )

    def come_b(k):
        at, other = plane(k)
        return pltpu.make_async_remote_copy(
            src_ref=buf_b.at[lax.div(at, 2)], dst_ref=buf_c.at[other, at],
            send_sem=ssem_b.at[k], recv_sem=rsem_b.at[at * 2 + other],
            device_id=plane_id(k), device_id_type=MESH,
        )

    @pl.loop(1, 2 * XY)
    def _(k):
        send_b(k).start()

    buf_c[core, xy] = buf_b[lax.div(xy, 2)]

    text_copy.wait()
    text[...] = text_pairs[...].reshape(2 * TEXT_PAD, D)
    text_row = iota((2 * TEXT_PAD, 2 * TEXT_PAD), 0)
    branch = jnp.where(text_row >= TEXT_PAD, 1, 0)
    part_text = onehot(
        iota((2 * TEXT_PAD, 2 * TEXT_PAD), 1) == (text_row - branch * TEXT_PAD) * 2 + branch
    )
    for c, out in ((0, tk_ref), (1, tv_ref)):
        projected = jnp.dot(text[...], w_split[c], preferred_element_type=F32)
        if c == 0:
            projected = jnp.concatenate(
                [
                    head_norm(projected[:, i * 128:(i + 1) * 128], gain_ref[2:3, :])
                    for i in range(SLABS)
                ],
                axis=1,
            )
        out[...] = (
            jnp.dot(part_text, projected.astype(BF16), preferred_element_type=F32)
            .astype(BF16).reshape(2, TEXT_PAD, WIDTH)
        )

    @pl.loop(1, 2 * XY)
    def _(k):
        come_b(k).wait_recv()

    for half in range(2):
        landed = buf_c[half].reshape(512, 128)
        for side, take in ((0, take_own), (1, take_par)):
            tiles = jnp.dot(take, landed, preferred_element_type=F32).astype(BF16)
            tok_ref[side, 2 * half] = tiles[:, :CH]
            tok_ref[side, 2 * half + 1] = tiles[:, CH:]

    mod_copy.wait_recv()
    modp_ref[...] = mod_s[...]

    @pl.loop(1, Z)
    def _(k):
        send_a(k).wait_send()

    @pl.loop(1, 2 * XY)
    def _(k):
        send_b(k).wait_send()

    mod_copy.wait_send()


def deal(latents, slots, mod, gains, text, w_text):
    anywhere = pl.BlockSpec(memory_space=pltpu.HBM)
    return pl.pallas_call(
        deal_kernel,
        out_shape=(
            jax.ShapeDtypeStruct((2, TILE, TILES, CH), BF16),
            jax.ShapeDtypeStruct((2, 2, D), F32),
            jax.ShapeDtypeStruct((2, TEXT_PAD, WIDTH), BF16),
            jax.ShapeDtypeStruct((2, TEXT_PAD, WIDTH), BF16),
        ),
        in_specs=[VMEM] * 4 + [anywhere] * 2,
        out_specs=(VMEM,) * 4,
        scratch_shapes=[
            pltpu.VMEM((Z, 32, 128), BF16),
            pltpu.VMEM((Z, 32, 128), BF16),
            pltpu.VMEM((Z, 32, 128), BF16),
            pltpu.VMEM((2, XY, 32, 128), BF16),
            pltpu.VMEM((2, 2, D), F32),
            pltpu.VMEM((TEXT_PAD, 2, D), BF16),
            pltpu.VMEM((2 * TEXT_PAD, D), BF16),
            pltpu.VMEM((D, 2, WIDTH), BF16),
            pltpu.VMEM((2, D, WIDTH), BF16),
            pltpu.SemaphoreType.DMA((Z,)),
            pltpu.SemaphoreType.DMA((Z,)),
            pltpu.SemaphoreType.DMA((2 * XY,)),
            pltpu.SemaphoreType.DMA((2 * XY,)),
            pltpu.SemaphoreType.DMA((2,)),
            pltpu.SemaphoreType.DMA((2,)),
        ],
        compiler_params=pltpu.CompilerParams(
            collective_id=0, has_side_effects=True, vmem_limit_bytes=40 << 20
        ),
        name="deal",
    )(latents, slots, mod, gains, text, w_text)


CHUNKS = ((0, 512), (512, 512), (1024, 512), (1536, 512), (2048, 384))


def home_kernel(
    att_ref, wout_ref, tok_ref, wemb_ref, wfin_ref, mod_ref, live_ref, lat_ref, slot_ref, out_ref,
    give, got, kept, hid, vel, buf_d, buf_e, buf_f, buf_g, xsend, xrecv, ssem_b, rsem_b, ssem_a, rsem_a,
):
    group, core, z, xy = where_am_i()
    other = 1 - core
    barrier = pltpu.get_barrier_semaphore()

    def z_id(k):
        return {"groups": z_peer(z, k) * XY + xy, "mp": core}

    def plane(k):
        return lax.rem(xy + k, XY)

    def plane_id(k):
        return {"groups": z * XY + plane(k), "mp": core}

    sibling = {"groups": group, "mp": other}
    pl.semaphore_signal(barrier, inc=1, device_id=sibling, device_id_type=MESH)

    @pl.loop(1, Z)
    def _(k):
        pl.semaphore_signal(barrier, inc=1, device_id=z_id(k), device_id_type=MESH)

    @pl.loop(1, XY)
    def _(k):
        pl.semaphore_signal(barrier, inc=1, device_id=plane_id(k), device_id_type=MESH)

    def exchange(b):
        return pltpu.make_async_remote_copy(
            src_ref=give.at[b], dst_ref=got.at[b], send_sem=xsend.at[b], recv_sem=xrecv.at[b],
            device_id=sibling, device_id_type=MESH,
        )

    def project(b, half, dst):
        rows = att_ref[b, half]
        for start, size in CHUNKS:
            dst[b, :, start:start + size] = jnp.dot(
                rows, wout_ref[:, start:start + size], preferred_element_type=F32
            ).astype(BF16)

    for b in range(2):
        project(b, other, give)
        if b == 0:
            pl.semaphore_wait(barrier, 1 + Z - 1 + XY - 1)
        exchange(b).start()
    for b in range(2):
        project(b, core, kept)
    for start, size in CHUNKS:
        hid[:, start:start + size] = jnp.dot(
            tok_ref[core], wemb_ref[:, start:start + size], preferred_element_type=F32
        )

    block = 48
    for b in range(2):
        exchange(b).wait_recv()
        gate, shift, scale = (mod_ref[i, b:b + 1, :] for i in (2, 3, 4))

        @pl.loop(0, HALF // block)
        def _(i):
            rows = pl.ds(pl.multiple_of(i * block, block), block)
            mixed = kept[b, rows, :].astype(F32) + got[b, rows, :].astype(F32)
            state = hid[rows, :] + gate * mixed
            centred = state - jnp.mean(state, axis=-1, keepdims=True)
            spread = jnp.mean(centred * centred, axis=-1, keepdims=True)
            final = (centred * lax.rsqrt(spread + EPS) * (1.0 + scale) + shift).astype(BF16)
            vel[b, rows, :] = lax.dot_general(
                final, wfin_ref[...], (((1,), (1,)), ((), ())), preferred_element_type=F32
            )

    guided = vel[1] + GUIDE * (vel[0] - vel[1])
    row = iota((HALF, CH), 0)
    upper = jnp.where(row >= TILES, 1, 0)
    position = (row - upper * TILES) * TILE + 2 * core + upper
    change = jnp.where(position < live_ref[group], STEP * guided, 0.0)
    change = jnp.concatenate([change[:TILES], change[TILES:]], axis=1).astype(BF16)

    row = iota((256, 1), 0)
    brought = landing(
        slot_ref, 256, (row & 7) * XY + (row >> 4), group.astype(F32), ((row >> 3) & 1).astype(F32)
    )
    spot = jnp.sum(brought, axis=1, keepdims=True)
    back = onehot(spot == iota((256, TILES), 1).astype(F32) + 1.0)
    buf_d[...] = (
        jnp.dot(back, change, preferred_element_type=F32).astype(BF16).reshape(XY, 16, 128)
    )

    def send_b(k):
        return pltpu.make_async_remote_copy(
            src_ref=buf_d.at[plane(k)], dst_ref=buf_e.at[xy],
            send_sem=ssem_b.at[k], recv_sem=rsem_b.at[xy],
            device_id=plane_id(k), device_id_type=MESH,
        )

    def come_b(k):
        return pltpu.make_async_remote_copy(
            src_ref=buf_d.at[plane(k)], dst_ref=buf_e.at[plane(k)],
            send_sem=ssem_b.at[k], recv_sem=rsem_b.at[plane(k)],
            device_id=plane_id(k), device_id_type=MESH,
        )

    @pl.loop(1, XY)
    def _(k):
        send_b(k).start()

    buf_e[xy] = buf_d[xy]
    out_row = iota((256, 256), 0)
    reorder = onehot(
        iota((256, 256), 1) == ((out_row >> 1) & 15) * 16 + (out_row & 1) * 8 + (out_row >> 5)
    )
    gather = onehot(iota((TILES, 256), 1).astype(F32) == my_buckets_column(slot_ref, group))

    @pl.loop(1, XY)
    def _(k):
        come_b(k).wait_recv()

    buf_f[...] = (
        jnp.dot(reorder, buf_e[...].reshape(256, 128), preferred_element_type=F32)
        .astype(BF16).reshape(Z, 32, 128)
    )

    def send_a(k):
        return pltpu.make_async_remote_copy(
            src_ref=buf_f.at[z_peer(z, k)], dst_ref=buf_g.at[z],
            send_sem=ssem_a.at[k], recv_sem=rsem_a.at[z],
            device_id=z_id(k), device_id_type=MESH,
        )

    def come_a(k):
        return pltpu.make_async_remote_copy(
            src_ref=buf_f.at[z_peer(z, k)], dst_ref=buf_g.at[z_peer(z, k)],
            send_sem=ssem_a.at[k], recv_sem=rsem_a.at[z_peer(z, k)],
            device_id=z_id(k), device_id_type=MESH,
        )

    @pl.loop(1, Z)
    def _(k):
        send_a(k).start()

    buf_g[z] = buf_f[z]

    @pl.loop(1, Z)
    def _(k):
        come_a(k).wait_recv()

    out_ref[...] = lat_ref[...] + jnp.dot(
        gather, buf_g[...].reshape(256, 128), preferred_element_type=F32
    )

    for b in range(2):
        exchange(b).wait_send()

    @pl.loop(1, XY)
    def _(k):
        send_b(k).wait_send()

    @pl.loop(1, Z)
    def _(k):
        send_a(k).wait_send()


def home(attended, w_out, tokens, w_embed, w_final, mod, live, latents, slots):
    return pl.pallas_call(
        home_kernel,
        out_shape=jax.ShapeDtypeStruct((TILES, 128), F32),
        in_specs=[VMEM] * 6 + [SMEM] + [VMEM] * 2,
        out_specs=VMEM,
        scratch_shapes=[
            pltpu.VMEM((2, HALF, D), BF16),
            pltpu.VMEM((2, HALF, D), BF16),
            pltpu.VMEM((2, HALF, D), BF16),
            pltpu.VMEM((HALF, D), F32),
            pltpu.VMEM((2, HALF, CH), F32),
            pltpu.VMEM((XY, 16, 128), BF16),
            pltpu.VMEM((XY, 16, 128), BF16),
            pltpu.VMEM((Z, 32, 128), BF16),
            pltpu.VMEM((Z, 32, 128), BF16),
            pltpu.SemaphoreType.DMA((2,)),
            pltpu.SemaphoreType.DMA((2,)),
            pltpu.SemaphoreType.DMA((XY,)),
            pltpu.SemaphoreType.DMA((XY,)),
            pltpu.SemaphoreType.DMA((Z,)),
            pltpu.SemaphoreType.DMA((Z,)),
        ],
        compiler_params=pltpu.CompilerParams(
            collective_id=1, has_side_effects=True, vmem_limit_bytes=40 << 20
        ),
        name="home",
    )(attended, w_out, tokens, w_embed, w_final, mod, live, latents, slots)


def token_position(shape):
    row = iota(shape, 0)
    quarter = sum(jnp.where(row >= TILES * j, 1, 0) for j in range(1, TILE))
    return (row - quarter * TILES) * TILE + quarter


def attend_kernel(
    tok_ref, wemb_ref, mod_ref, modp_ref, w_hbm, tk_ref, tv_ref, gain_ref, live_ref, partner_ref,
    out_ref, wbuf, normed, qbuf, kbuf, vbuf, wsem,
):
    group = lax.axis_index("groups")
    mate = partner_ref[group]
    own_len = live_ref[group]
    mate_len = jnp.where(mate != group, live_ref[mate], 0)

    def fetch(c):
        return pltpu.make_async_copy(w_hbm.at[c], wbuf.at[c], wsem.at[c])

    for c in (1, 2, 0):
        fetch(c).start()

    block = 96
    for side, source in ((0, mod_ref), (1, modp_ref)):
        @pl.loop(0, ROWS // block)
        def _(i):
            rows = pl.ds(pl.multiple_of(i * block, block), block)
            hidden = jnp.dot(tok_ref[side, rows, :], wemb_ref[...], preferred_element_type=F32)
            centred = hidden - jnp.mean(hidden, axis=-1, keepdims=True)
            spread = jnp.mean(centred * centred, axis=-1, keepdims=True)
            scaled = centred * lax.rsqrt(spread + EPS)
            for b in range(2):
                normed[2 * side + b, rows, :] = (
                    scaled * (1.0 + source[1, b:b + 1, :]) + source[0, b:b + 1, :]
                ).astype(BF16)

    slot = token_position((ROWS, 128))
    text_pad = iota((TEXT_PAD, 128), 0) < TEXT
    for b in range(2):
        for s in range(SLABS):
            lanes = slice(s * 128, (s + 1) * 128)
            first = jnp.broadcast_to(tk_ref[b, 0:1, lanes], (TEXT_PAD, 128))
            kbuf[b, s, 2 * ROWS:, :] = jnp.where(text_pad, tk_ref[b, :, lanes], first)
            vbuf[b, s, 2 * ROWS:, :128] = tv_ref[b, :, lanes]
            vbuf[b, s, 2 * ROWS:, 128:] = onehot(text_pad)

    fetch(1).wait()

    @pl.loop(0, 4)
    def _(n):
        side, b = lax.div(n, 2), lax.rem(n, 2)
        usable = slot < jnp.where(side == 0, own_len, mate_len)
        rows = pl.ds(pl.multiple_of(side * ROWS, ROWS), ROWS)
        keys = jnp.dot(normed[n], wbuf[1], preferred_element_type=F32)
        for s in range(SLABS):
            lanes = slice(s * 128, (s + 1) * 128)
            key = head_norm(keys[:, lanes], gain_ref[1:2, :]).astype(BF16)
            first = jnp.broadcast_to(tk_ref[b, 0:1, lanes], (ROWS, 128))
            kbuf[b, s, rows, :] = jnp.where(usable, key, first)

    fetch(2).wait()

    @pl.loop(0, 4)
    def _(n):
        side, b = lax.div(n, 2), lax.rem(n, 2)
        usable = slot < jnp.where(side == 0, own_len, mate_len)
        rows = pl.ds(pl.multiple_of(side * ROWS, ROWS), ROWS)
        values = jnp.dot(normed[n], wbuf[2], preferred_element_type=F32)
        for s in range(SLABS):
            value = values[:, s * 128:(s + 1) * 128]
            vbuf[b, s, rows, :128] = jnp.where(usable, value, 0.0).astype(BF16)
            vbuf[b, s, rows, 128:] = onehot(usable)

    fetch(0).wait()

    @pl.loop(0, 2)
    def _(b):
        query = jnp.dot(normed[b], wbuf[0], preferred_element_type=F32)
        for s in range(SLABS):
            qbuf[b, s] = head_norm(query[:, s * 128:(s + 1) * 128], gain_ref[0:1, :]).astype(BF16)

    lower = iota((ROWS, 128), 1) < HEAD

    @pl.loop(0, 2 * SLABS)
    def _(n):
        b, s = lax.div(n, SLABS), lax.rem(n, SLABS)
        query, key, value = qbuf[b, s], kbuf[b, s], vbuf[b, s]
        parts = []
        for mine in (lower, ~lower):
            scores = lax.dot_general(
                jnp.where(mine, query, jnp.zeros_like(query)), key, (((1,), (1,)), ((), ())),
                preferred_element_type=F32,
            )
            highest = jnp.max(scores, axis=-1, keepdims=True)
            raised = jnp.exp((scores - highest) * HEAD ** (-0.5)).astype(BF16)
            both = jnp.dot(raised, value, preferred_element_type=F32)
            parts.append(both[:, :128] / both[:, 128:])
        out_ref[b, :, pl.ds(pl.multiple_of(s * 128, 128), 128)] = (
            jnp.where(lower, parts[0], parts[1]).astype(BF16)
        )


def attend(tokens, w_embed, mod, mod_mate, w_qkv, text_key, text_value, gains, live, partner):
    return pl.pallas_call(
        attend_kernel,
        out_shape=jax.ShapeDtypeStruct((2, ROWS, WIDTH), BF16),
        in_specs=[VMEM] * 4 + [pl.BlockSpec(memory_space=pltpu.HBM)] + [VMEM] * 3 + [SMEM] * 2,
        out_specs=VMEM,
        scratch_shapes=[
            pltpu.VMEM((3, D, WIDTH), BF16),
            pltpu.VMEM((4, ROWS, D), BF16),
            pltpu.VMEM((2, SLABS, ROWS, 128), BF16),
            pltpu.VMEM((2, SLABS, KEYS, 128), BF16),
            pltpu.VMEM((2, SLABS, KEYS, 256), BF16),
            pltpu.SemaphoreType.DMA((3,)),
        ],
        compiler_params=pltpu.CompilerParams(vmem_limit_bytes=48 << 20),
        name="attend",
    )(tokens, w_embed, mod, mod_mate, w_qkv, text_key, text_value, gains, live, partner)


def shards(
    latents, tile_slot, live, partner, text_states, modulation,
    w_embed, w_qkv, w_text_kv, w_out, w_final, norm_gains,
):
    slots = tile_slot.reshape(Z * XY, TILES)
    mod = modulation[0].transpose(1, 0, 2)
    gains = jnp.concatenate([norm_gains, norm_gains], axis=1)
    tokens, mod_mate, text_key, text_value = deal(
        latents, slots, mod, gains, text_states[0].transpose(1, 0, 2), w_text_kv
    )
    tokens = tokens.reshape(2, ROWS, CH)
    attended = attend(
        tokens, w_embed, mod, mod_mate, w_qkv.transpose(1, 0, 2), text_key, text_value,
        gains, live, partner,
    )
    return home(
        attended.reshape(2, 2, HALF, WIDTH), w_out, tokens[0].reshape(2, HALF, CH),
        w_embed, w_final.T, mod, live, latents, slots,
    )


def solution(mesh):
    placed = (
        P("groups", "mp"), P(), P(), P(),
        P("groups", None, None, None), P("groups", None, None, None),
        P(), P(None, None, "mp"), P(None, None, "mp"), P("mp", None), P(), P(),
    )
    return jax.shard_map(
        shards, mesh=mesh, in_specs=placed, out_specs=P("groups", "mp"), check_vma=False
    )
```

```python
import functools
import jax
import jax.numpy as jnp
from jax import lax
from jax.experimental import pallas as pl
from jax.experimental.pallas import tpu as pltpu
from jax.sharding import PartitionSpec as P

HEAD = 64
CH = 64
TEXT = 154
TEXT_PAD = 160
ROWS = 384
HALF = ROWS // 2
TILE = 4
TILES = 96
D = 2432
Z = 8
XY = 16
KEYS = 2 * ROWS + TEXT_PAD
WIDTH = 640
SLABS = WIDTH // 128
CHUNKS = ((0, 512), (512, 512), (1024, 512), (1536, 512), (2048, 384))

GUIDE = 3.5
STEP = -0.25
EPS = 1e-06
LOG2E = 1.4426950408889634
F32 = jnp.float32
BF16 = jnp.bfloat16
MESH = pl.DeviceIdType.MESH
NT = (((1,), (1,)), ((), ()))


def iota(shape, axis):
    return lax.broadcasted_iota(jnp.int32, shape, axis)


def onehot(condition):
    return jnp.where(condition, 1.0, 0.0).astype(BF16)


def dot(left, right):
    return jnp.dot(left, right, preferred_element_type=F32)


def group_of(slot):
    return (slot * 43691) >> 22


def head_norm(slab, gains):
    square = slab * slab
    lower = iota(slab.shape, 1) < HEAD
    first = jnp.sum(jnp.where(lower, square, 0.0), axis=-1, keepdims=True) * (1.0 / HEAD)
    second = jnp.sum(jnp.where(lower, 0.0, square), axis=-1, keepdims=True) * (1.0 / HEAD)
    return slab * jnp.where(lower, lax.rsqrt(first + EPS), lax.rsqrt(second + EPS)) * gains


def step_kernel(
    lat_hbm, slot_hbm, mod_hbm, gain_hbm, text_hbm, wtext_hbm, wemb_hbm, wqkv_hbm, wout_hbm,
    wfin_hbm, live_ref, partner_ref, out_ref,
    lat, slot_raw, slot_tab, mod, mod_mate, gain, text_pairs, text, w_pairs, w_split, wemb, wqkv,
    wout, wfin, tk, tv, tok, normed, qbuf, kbuf, vbuf, att, got, hid, vel,
    out_a, in_a, out_b, in_b, home_b, back_b, home_a, back_a,
    lsem, msem, ssem_a, rsem_a, ssem_b, rsem_b, ssem_c, rsem_c, xsend, xrecv,
    hsend_b, hrecv_b, hsend_a, hrecv_a,
):
    group, core = lax.axis_index("groups"), lax.axis_index("mp")
    z, xy = lax.div(group, XY), lax.rem(group, XY)
    other = 1 - core
    mate = group + 1 - 2 * lax.rem(group, 2)
    sibling_id = {"groups": group, "mp": other}
    mate_id = {"groups": mate, "mp": core}
    cross_id = {"groups": mate, "mp": other}

    def z_peer(k):
        return lax.rem(z + k, Z)

    def z_id(k):
        return {"groups": z_peer(k) * XY + xy, "mp": core}

    def plane_peer(k):
        return lax.rem(xy + k, XY)

    def plane_id(k):
        return {"groups": z * XY + plane_peer(k), "mp": core}

    def remote(src, dst, send, recv, to):
        return pltpu.make_async_remote_copy(
            src_ref=src, dst_ref=dst, send_sem=send, recv_sem=recv,
            device_id=to, device_id_type=MESH,
        )

    barrier = pltpu.get_barrier_semaphore()

    @pl.loop(1, Z)
    def _(k):
        pl.semaphore_signal(barrier, inc=1, device_id=z_id(k), device_id_type=MESH)

    @pl.loop(1, XY)
    def _(k):
        pl.semaphore_signal(barrier, inc=1, device_id=plane_id(k), device_id_type=MESH)

    for to in (sibling_id, cross_id):
        pl.semaphore_signal(barrier, inc=1, device_id=to, device_id_type=MESH)

    loads = [
        (slot_hbm, slot_raw), (lat_hbm, lat), (text_hbm, text_pairs.at[pl.ds(0, TEXT)]),
        (wtext_hbm, w_pairs), (gain_hbm, gain), (mod_hbm, mod), (wemb_hbm, wemb),
    ] + [
        (wqkv_hbm.at[c], wqkv.at[:, pl.ds(c * WIDTH, WIDTH)]) for c in range(3)
    ] + [(wout_hbm, wout), (wfin_hbm, wfin)]
    loads = [
        pltpu.make_async_copy(src, dst, lsem.at[i]) for i, (src, dst) in enumerate(loads)
    ]
    (slot_load, lat_load, text_load, wtext_load, gain_load, mod_load, wemb_load,
     q_load, k_load, v_load, wout_load, wfin_load) = loads
    for load in loads:
        load.start()
    text_pairs[TEXT:] = jnp.zeros((TEXT_PAD - TEXT, 2, D), BF16)

    slot_load.wait()
    three = jnp.concatenate([slot_raw[pl.ds(i, 32, stride=3), :] for i in range(3)], axis=1)
    for k in range(4):
        slot_tab[32 * k:32 * (k + 1), :] = three[:, TILES * k:TILES * (k + 1)]

    mine = slot_tab[pl.ds(lax.rem(group, 4) * 32 + lax.div(group, 4), 1), :]
    mine = jnp.broadcast_to(group_of(mine).astype(F32), (TILES, TILES))
    across, down = iota((TILES, TILES), 1), iota((TILES, TILES), 0)
    column = jnp.sum(jnp.where(across == down, mine, 0.0), axis=1, keepdims=True)
    same = mine == column
    bucket_row = 2.0 * mine[:1] + jnp.sum(
        jnp.where(same & (down < across), 1.0, 0.0), axis=0, keepdims=True
    )
    bucket_column = 2.0 * column + jnp.sum(
        jnp.where(same & (across < down), 1.0, 0.0), axis=1, keepdims=True
    )
    sender = onehot(iota((256, TILES), 0).astype(F32) == bucket_row)
    lat_load.wait()
    out_a[...] = dot(sender, lat[...].astype(BF16)).astype(BF16).reshape(Z, 32, 128)

    pl.semaphore_wait(barrier, Z - 1 + XY - 1 + 2)

    def send_a(k):
        return remote(out_a.at[z_peer(k)], in_a.at[z], ssem_a.at[k], rsem_a.at[z], z_id(k))

    def come_a(k):
        at = z_peer(k)
        return remote(out_a.at[at], in_a.at[at], ssem_a.at[k], rsem_a.at[at], z_id(k))

    @pl.loop(1, Z)
    def _(k):
        send_a(k).start()

    mod_copy = remote(mod_hbm.at[pl.ds(0, 2)], mod_mate, msem.at[0], msem.at[1], mate_id)
    mod_copy.start()
    in_a[z] = out_a[z]

    part_row = iota((256, 256), 0)
    part = onehot(iota((256, 256), 1) == (part_row & 127) * 2 + (part_row >> 7))
    wtext_load.wait()

    @pl.loop(0, D // 128)
    def _(i):
        rows = pl.ds(pl.multiple_of(i * 128, 128), 128)
        both = dot(part, w_pairs[rows].reshape(256, WIDTH))
        w_split[0, rows, :] = both[:128].astype(BF16)
        w_split[1, rows, :] = both[128:].astype(BF16)

    @pl.loop(1, Z)
    def _(k):
        come_a(k).wait_recv()

    row, col = iota((256, 256), 0), iota((256, 256), 1)
    reorder = onehot(col == (row & 7) * 32 + (row >> 4) * 2 + ((row >> 3) & 1))
    out_b[...] = dot(reorder, in_a[...].reshape(256, 128)).astype(BF16).reshape(XY, 16, 128)

    def send_b(k):
        return remote(out_b.at[plane_peer(k)], in_b.at[xy], ssem_b.at[k], rsem_b.at[xy], plane_id(k))

    def come_b(k):
        at = plane_peer(k)
        return remote(out_b.at[at], in_b.at[at], ssem_b.at[k], rsem_b.at[at], plane_id(k))

    @pl.loop(1, XY)
    def _(k):
        send_b(k).start()

    in_b[xy] = out_b[xy]

    slot = slot_tab[...]
    target = group_of(slot)
    placed = slot - target * TILES
    row = iota((256, 1), 0)
    pick = onehot(
        iota((256, Z * XY), 1) == ((row >> 4) & 3) * 32 + (row & 7) * 4 + (row >> 6)
    )
    goal = dot(pick, target.astype(F32).astype(BF16))
    place = dot(pick, placed.astype(F32).astype(BF16))
    matched = jnp.where(goal == group.astype(F32), 1.0, 0.0)
    before = onehot(iota((TILES, TILES), 0) < iota((TILES, TILES), 1))
    rank = dot(matched.astype(BF16), before)
    brought = jnp.where(
        (matched > 0.5) & (rank == ((row >> 3) & 1).astype(F32)), place + 1.0, 0.0
    )
    spot_row = lax.dot_general(
        jnp.ones((8, TILES), BF16), brought.astype(BF16), NT, preferred_element_type=F32
    )[:1]
    spot_column = jnp.sum(brought, axis=1, keepdims=True)
    settle = onehot(iota((TILES, 256), 0).astype(F32) + 1.0 == spot_row)

    text_load.wait()
    gain_load.wait()
    text[...] = text_pairs[...].reshape(2 * TEXT_PAD, D)
    text_row, text_col = (iota((2 * TEXT_PAD, 2 * TEXT_PAD), i) for i in range(2))
    branch = jnp.where(text_row >= TEXT_PAD, 1, 0)
    part_text = onehot(text_col == (text_row - branch * TEXT_PAD) * 2 + branch)

    def project_text(c, out):
        projected = dot(text[...], w_split[c])
        if c == 0:
            slabs = [
                head_norm(projected[:, i * 128:(i + 1) * 128], gain[2:3, :]) for i in range(SLABS)
            ]
            projected = jnp.concatenate(slabs, axis=1)
        out[...] = dot(part_text, projected.astype(BF16)).astype(BF16).reshape(2, TEXT_PAD, WIDTH)

    project_text(0, tk)

    @pl.loop(1, XY)
    def _(k):
        come_b(k).wait_recv()

    tok[0, core] = dot(settle, in_b[...].reshape(256, 128)).astype(BF16)

    def send_c(i):
        side, to = ((1, mate_id), (0, sibling_id), (1, cross_id))[i]
        return remote(tok.at[0, core], tok.at[side, core], ssem_c.at[i], rsem_c.at[i], to)

    def come_c(i):
        side, half, to = ((1, core, mate_id), (0, other, sibling_id), (1, other, cross_id))[i]
        return remote(tok.at[0, core], tok.at[side, half], ssem_c.at[i], rsem_c.at[i], to)

    for i in range(3):
        send_c(i).start()

    project_text(1, tv)
    text_used = iota((TEXT_PAD, 128), 0) < TEXT
    for b in range(2):
        for s in range(SLABS):
            lanes = slice(s * 128, (s + 1) * 128)
            first = jnp.broadcast_to(tk[b, 0:1, lanes], (TEXT_PAD, 128))
            kbuf[b, s, 2 * ROWS:, :] = jnp.where(text_used, tk[b, :, lanes], first)
            vbuf[b, s, 2 * ROWS:, :128] = tv[b, :, lanes]
            vbuf[b, s, 2 * ROWS:, 128:] = onehot(text_used)

    own_len = live_ref[group]
    mate_len = jnp.where(partner_ref[group] != group, live_ref[mate], 0)
    row = iota((ROWS, 128), 0)
    quarter = sum(jnp.where(row >= TILES * j, 1, 0) for j in range(1, TILE))
    position = (row - quarter * TILES) * TILE + quarter

    for load in (mod_load, wemb_load, q_load, k_load, v_load):
        load.wait()
    for i in range(3):
        come_c(i).wait_recv()
    mod_copy.wait_recv()

    def embed(side, half, source):
        for low in range(2):
            piece = tok[side, half][:, low * CH:(low + 1) * CH]
            hidden = dot(piece, wemb[...])
            centred = hidden - jnp.mean(hidden, axis=-1, keepdims=True)
            spread = jnp.mean(centred * centred, axis=-1, keepdims=True)
            scaled = centred * lax.rsqrt(spread + EPS)
            rows = pl.ds(pl.multiple_of((2 * half + low) * TILES, 32), TILES)
            for b in range(2):
                normed[2 * side + b, rows, :] = (
                    scaled * (1.0 + source[1, b:b + 1, :]) + source[0, b:b + 1, :]
                ).astype(BF16)

    def put(side, b, slab_index, slab):
        usable = position < (own_len if side == 0 else mate_len)
        rows = slice(side * ROWS, (side + 1) * ROWS)
        c, s = divmod(slab_index, SLABS)
        if c == 0:
            qbuf[b, s] = head_norm(slab, gain[0:1, :]).astype(BF16)
        elif c == 1:
            key = head_norm(slab, gain[1:2, :]).astype(BF16)
            first = jnp.broadcast_to(tk[b, 0:1, s * 128:(s + 1) * 128], key.shape)
            kbuf[b, s, rows, :] = jnp.where(usable, key, first)
        else:
            vbuf[b, s, rows, :128] = jnp.where(usable, slab, 0.0).astype(BF16)
            vbuf[b, s, rows, 128:] = onehot(usable)

    def project(side, b, slabs):
        for i in range(0, len(slabs), 2):
            pair = slabs[i:i + 2]
            out = dot(normed[2 * side + b], wqkv[:, pair[0] * 128:(pair[-1] + 1) * 128])
            for t, slab_index in enumerate(pair):
                put(side, b, slab_index, out[:, t * 128:(t + 1) * 128])

    @pl.loop(0, 2)
    def _(half):
        embed(0, half, mod)

    @pl.loop(0, 2)
    def _(b):
        project(0, b, list(range(3 * SLABS)))
        embed(1, b, mod_mate)

    @pl.loop(0, 2)
    def _(b):
        project(1, b, list(range(SLABS, 3 * SLABS)))

    def half_rows(b):
        return slice(b * HALF, (b + 1) * HALF) if isinstance(b, int) else pl.ds(
            pl.multiple_of(b * HALF, HALF), HALF
        )

    def exchange(b):
        return remote(
            normed.at[0, half_rows(b)], got.at[b], xsend.at[b], xrecv.at[b], sibling_id
        )

    def project_out(b, half, into):
        rows = att[b, pl.ds(pl.multiple_of(half * HALF, HALF), HALF), :]
        for start, size in CHUNKS:
            normed[into, half_rows(b), start:start + size] = dot(
                rows, wout[:, start:start + size]
            ).astype(BF16)

    lower = iota((ROWS, 128), 1) < HEAD
    wout_load.wait()

    @pl.loop(0, 2)
    def _(b):
        for s in range(SLABS):
            query, key, value = qbuf[b, s], kbuf[b, s], vbuf[b, s]
            parts = []
            for head in (lower, ~lower):
                scores = lax.dot_general(
                    jnp.where(head, query, jnp.zeros_like(query)), key, NT,
                    preferred_element_type=F32,
                )
                highest = jnp.max(scores, axis=-1, keepdims=True)
                raised = jnp.exp2((scores - highest) * (HEAD ** (-0.5) * LOG2E)).astype(BF16)
                both = dot(raised, value)
                parts.append(both[:, :128] / both[:, 128:])
            att[b, :, s * 128:(s + 1) * 128] = jnp.where(lower, parts[0], parts[1]).astype(BF16)
        project_out(b, other, 0)
        exchange(b).start()

    wfin_load.wait()
    for b in range(2):
        project_out(b, core, 1)
    for low in range(2):
        piece = tok[0, core][:, low * CH:(low + 1) * CH]
        for start, size in CHUNKS:
            hid[low * TILES:(low + 1) * TILES, start:start + size] = dot(
                piece, wemb[:, start:start + size]
            )

    block = 48
    for b in range(2):
        exchange(b).wait_recv()
        gate, shift, scale = (mod[i, b:b + 1, :] for i in (2, 3, 4))

        @pl.loop(0, HALF // block)
        def _(i):
            rows = pl.ds(pl.multiple_of(i * block, block), block)
            kept = normed[1, pl.ds(pl.multiple_of(b * HALF + i * block, block), block), :]
            mixed = kept.astype(F32) + got[b, rows, :].astype(F32)
            state = hid[rows, :] + gate * mixed
            centred = state - jnp.mean(state, axis=-1, keepdims=True)
            spread = jnp.mean(centred * centred, axis=-1, keepdims=True)
            final = (centred * lax.rsqrt(spread + EPS) * (1.0 + scale) + shift).astype(BF16)
            vel[b, rows, :] = lax.dot_general(final, wfin[...], NT, preferred_element_type=F32)

    guided = vel[1] + GUIDE * (vel[0] - vel[1])
    row = iota((HALF, CH), 0)
    upper = jnp.where(row >= TILES, 1, 0)
    position = (row - upper * TILES) * TILE + 2 * core + upper
    change = jnp.where(position < own_len, STEP * guided, 0.0)
    change = jnp.concatenate([change[:TILES], change[TILES:]], axis=1).astype(BF16)
    unsettle = onehot(spot_column == iota((256, TILES), 1).astype(F32) + 1.0)
    home_b[...] = dot(unsettle, change).astype(BF16).reshape(XY, 16, 128)

    def return_b(k):
        return remote(
            home_b.at[plane_peer(k)], back_b.at[xy], hsend_b.at[k], hrecv_b.at[xy], plane_id(k)
        )

    def arrive_b(k):
        at = plane_peer(k)
        return remote(home_b.at[at], back_b.at[at], hsend_b.at[k], hrecv_b.at[at], plane_id(k))

    @pl.loop(1, XY)
    def _(k):
        return_b(k).start()

    back_b[xy] = home_b[xy]
    row, col = iota((256, 256), 0), iota((256, 256), 1)
    reorder = onehot(col == ((row >> 1) & 15) * 16 + (row & 1) * 8 + (row >> 5))
    collect = onehot(iota((TILES, 256), 1).astype(F32) == bucket_column)

    @pl.loop(1, XY)
    def _(k):
        arrive_b(k).wait_recv()

    home_a[...] = dot(reorder, back_b[...].reshape(256, 128)).astype(BF16).reshape(Z, 32, 128)

    def return_a(k):
        return remote(
            home_a.at[z_peer(k)], back_a.at[z], hsend_a.at[k], hrecv_a.at[z], z_id(k)
        )

    def arrive_a(k):
        at = z_peer(k)
        return remote(home_a.at[at], back_a.at[at], hsend_a.at[k], hrecv_a.at[at], z_id(k))

    @pl.loop(1, Z)
    def _(k):
        return_a(k).start()

    back_a[z] = home_a[z]

    @pl.loop(1, Z)
    def _(k):
        send_a(k).wait_send()

    @pl.loop(1, XY)
    def _(k):
        send_b(k).wait_send()
        return_b(k).wait_send()

    for i in range(3):
        send_c(i).wait_send()
    mod_copy.wait_send()
    for b in range(2):
        exchange(b).wait_send()

    @pl.loop(1, Z)
    def _(k):
        arrive_a(k).wait_recv()

    out_ref[...] = lat[...] + dot(collect, back_a[...].reshape(256, 128))

    @pl.loop(1, Z)
    def _(k):
        return_a(k).wait_send()


def step(*operands):
    hbm = pl.BlockSpec(memory_space=pltpu.HBM)
    smem = pl.BlockSpec(memory_space=pltpu.SMEM)
    narrow, wide = pltpu.VMEM((Z, 32, 128), BF16), pltpu.VMEM((XY, 16, 128), BF16)
    dma = pltpu.SemaphoreType.DMA
    return pl.pallas_call(
        step_kernel,
        out_shape=jax.ShapeDtypeStruct((TILES, 128), F32),
        in_specs=[hbm] * 10 + [smem] * 2,
        out_specs=pl.BlockSpec(memory_space=pltpu.VMEM),
        scratch_shapes=[
            pltpu.VMEM((TILES, 128), F32),
            pltpu.VMEM((TILES, 128), jnp.int32),
            pltpu.VMEM((Z * XY, TILES), jnp.int32),
            pltpu.VMEM((5, 2, D), F32),
            pltpu.VMEM((2, 2, D), F32),
            pltpu.VMEM((3, 128), F32),
            pltpu.VMEM((TEXT_PAD, 2, D), BF16),
            pltpu.VMEM((2 * TEXT_PAD, D), BF16),
            pltpu.VMEM((D, 2, WIDTH), BF16),
            pltpu.VMEM((2, D, WIDTH), BF16),
            pltpu.VMEM((CH, D), BF16),
            pltpu.VMEM((D, 3 * WIDTH), BF16),
            pltpu.VMEM((WIDTH, D), BF16),
            pltpu.VMEM((CH, D), BF16),
            pltpu.VMEM((2, TEXT_PAD, WIDTH), BF16),
            pltpu.VMEM((2, TEXT_PAD, WIDTH), BF16),
            pltpu.VMEM((2, 2, TILES, 128), BF16),
            pltpu.VMEM((4, ROWS, D), BF16),
            pltpu.VMEM((2, SLABS, ROWS, 128), BF16),
            pltpu.VMEM((2, SLABS, KEYS, 128), BF16),
            pltpu.VMEM((2, SLABS, KEYS, 256), BF16),
            pltpu.VMEM((2, ROWS, WIDTH), BF16),
            pltpu.VMEM((2, HALF, D), BF16),
            pltpu.VMEM((HALF, D), F32),
            pltpu.VMEM((2, HALF, CH), F32),
            narrow, narrow, wide, wide, wide, wide, narrow, narrow,
            dma((12,)), dma((2,)), dma((Z,)), dma((Z,)), dma((XY,)), dma((XY,)),
            dma((3,)), dma((3,)), dma((2,)), dma((2,)),
            dma((XY,)), dma((XY,)), dma((Z,)), dma((Z,)),
        ],
        compiler_params=pltpu.CompilerParams(
            collective_id=0, has_side_effects=True, vmem_limit_bytes=62 << 20
        ),
        name="step",
    )(*operands)


def shards(
    latents, tile_slot, live, partner, text_states, modulation,
    w_embed, w_qkv, w_text_kv, w_out, w_final, norm_gains,
):
    return step(
        latents, tile_slot.reshape(TILES, 128), modulation[0].transpose(1, 0, 2),
        jnp.concatenate([norm_gains, norm_gains], axis=1), text_states[0].transpose(1, 0, 2),
        w_text_kv, w_embed, w_qkv.transpose(1, 0, 2), w_out, w_final.T, live, partner,
    )


def solution(mesh):
    placed = (
        P("groups", "mp"), P(), P(), P(),
        P("groups", None, None, None), P("groups", None, None, None),
        P(), P(None, None, "mp"), P(None, None, "mp"), P("mp", None), P(), P(),
    )
    return jax.shard_map(
        shards, mesh=mesh, in_specs=placed, out_specs=P("groups", "mp"), check_vma=False
    )
```

```python
import functools
import jax
import jax.numpy as jnp
from jax import lax
from jax.experimental import pallas as pl
from jax.experimental.pallas import tpu as pltpu
from jax.sharding import PartitionSpec as P

HEAD = 64
CH = 64
TEXT = 154
TEXT_PAD = 160
ROWS = 384
HALF = ROWS // 2
TILE = 4
TILES = 96
D = 2432
Z = 8
XY = 16
KEYS = 2 * ROWS + TEXT_PAD
WIDTH = 640
SLABS = WIDTH // 128
CHUNKS = ((0, 512), (512, 512), (1024, 512), (1536, 512), (2048, 384))

GUIDE = 3.5
STEP = -0.25
EPS = 1e-06
LOG2E = 1.4426950408889634
F32 = jnp.float32
BF16 = jnp.bfloat16
MESH = pl.DeviceIdType.MESH
NT = (((1,), (1,)), ((), ()))


def iota(shape, axis):
    return lax.broadcasted_iota(jnp.int32, shape, axis)


def onehot(condition):
    return jnp.where(condition, 1.0, 0.0).astype(BF16)


def dot(left, right):
    return jnp.dot(left, right, preferred_element_type=F32)


def group_of(slot):
    return (slot * 43691) >> 22


def head_norm(slab, gains):
    square = slab * slab
    lower = iota(slab.shape, 1) < HEAD
    first = jnp.sum(jnp.where(lower, square, 0.0), axis=-1, keepdims=True) * (1.0 / HEAD)
    second = jnp.sum(jnp.where(lower, 0.0, square), axis=-1, keepdims=True) * (1.0 / HEAD)
    return slab * jnp.where(lower, lax.rsqrt(first + EPS), lax.rsqrt(second + EPS)) * gains


def step_kernel(
    lat_hbm, slot_hbm, mod_hbm, gain_hbm, text_hbm, wtext_hbm, wemb_hbm, wqkv_hbm, wout_hbm,
    wfin_hbm, live_ref, partner_ref, out_ref,
    lat, slot_raw, slot_tab, mod, mod_mate, gain_half, gain, text_pairs, text, w_pairs, w_split, wemb, wqkv,
    wout, wfin, tk, tv, tok, normed, qbuf, kbuf, vbuf, att, got, hid, line, vel, landing,
    out_a, in_a, out_b, in_b, home_b, back_b, home_a, back_a,
    lsem, msem, ssem_a, rsem_a, ssem_b, rsem_b, ssem_c, rsem_c, xsend, xrecv,
    hsend_b, hrecv_b, hsend_a, hrecv_a,
):
    group, core = lax.axis_index("groups"), lax.axis_index("mp")
    z, xy = lax.div(group, XY), lax.rem(group, XY)
    other = 1 - core
    mate = group + 1 - 2 * lax.rem(group, 2)
    sibling_id = {"groups": group, "mp": other}
    mate_id = {"groups": mate, "mp": core}

    def z_peer(k):
        return lax.rem(z + k, Z)

    def z_id(k):
        return {"groups": z_peer(k) * XY + xy, "mp": core}

    def plane_peer(k):
        return lax.rem(xy + k, XY)

    def plane_id(k):
        return {"groups": z * XY + plane_peer(k), "mp": core}

    def remote(src, dst, send, recv, to):
        return pltpu.make_async_remote_copy(
            src_ref=src, dst_ref=dst, send_sem=send, recv_sem=recv,
            device_id=to, device_id_type=MESH,
        )

    barrier = pltpu.get_barrier_semaphore()

    @pl.loop(1, Z)
    def _(k):
        pl.semaphore_signal(barrier, inc=1, device_id=z_id(k), device_id_type=MESH)

    @pl.loop(1, XY)
    def _(k):
        pl.semaphore_signal(barrier, inc=1, device_id=plane_id(k), device_id_type=MESH)

    pl.semaphore_signal(barrier, inc=1, device_id=sibling_id, device_id_type=MESH)

    loads = [
        (slot_hbm, slot_raw), (lat_hbm, lat), (text_hbm, text_pairs.at[pl.ds(0, TEXT)]),
        (wtext_hbm, w_pairs), (gain_hbm, gain_half), (mod_hbm, mod), (wemb_hbm, wemb),
    ] + [
        (wqkv_hbm.at[c], wqkv.at[:, pl.ds(c * WIDTH, WIDTH)]) for c in range(3)
    ] + [(wout_hbm, wout), (wfin_hbm, wfin)]
    loads = [
        pltpu.make_async_copy(src, dst, lsem.at[i]) for i, (src, dst) in enumerate(loads)
    ]
    (slot_load, lat_load, text_load, wtext_load, gain_load, mod_load, wemb_load,
     q_load, k_load, v_load, wout_load, wfin_load) = loads
    for load in loads:
        load.start()
    text_pairs[TEXT:] = jnp.zeros((TEXT_PAD - TEXT, 2, D), BF16)

    slot_load.wait()
    three = jnp.concatenate([slot_raw[pl.ds(i, 32, stride=3), :] for i in range(3)], axis=1)
    for k in range(4):
        slot_tab[32 * k:32 * (k + 1), :] = three[:, TILES * k:TILES * (k + 1)]

    mine = slot_tab[pl.ds(lax.rem(group, 4) * 32 + lax.div(group, 4), 1), :]
    mine = jnp.broadcast_to(group_of(mine).astype(F32), (TILES, TILES))
    across, down = iota((TILES, TILES), 1), iota((TILES, TILES), 0)
    column = jnp.sum(jnp.where(across == down, mine, 0.0), axis=1, keepdims=True)
    same = mine == column
    bucket_row = 2.0 * mine[:1] + jnp.sum(
        jnp.where(same & (down < across), 1.0, 0.0), axis=0, keepdims=True
    )
    bucket_column = 2.0 * column + jnp.sum(
        jnp.where(same & (across < down), 1.0, 0.0), axis=1, keepdims=True
    )
    sender = onehot(iota((256, TILES), 0).astype(F32) == bucket_row)
    lat_load.wait()
    out_a[...] = dot(sender, lat[...].astype(BF16)).astype(BF16).reshape(Z, 32, 128)

    pl.semaphore_wait(barrier, Z - 1 + XY - 1 + 1)

    def send_a(k):
        return remote(out_a.at[z_peer(k)], in_a.at[z], ssem_a.at[k], rsem_a.at[z], z_id(k))

    def come_a(k):
        at = z_peer(k)
        return remote(out_a.at[at], in_a.at[at], ssem_a.at[k], rsem_a.at[at], z_id(k))

    @pl.loop(1, Z)
    def _(k):
        send_a(k).start()

    mod_copy = remote(mod_hbm.at[pl.ds(0, 2)], mod_mate, msem.at[0], msem.at[1], mate_id)
    mod_copy.start()
    in_a[z] = out_a[z]

    part_row = iota((256, 256), 0)
    part = onehot(iota((256, 256), 1) == (part_row & 127) * 2 + (part_row >> 7))
    wtext_load.wait()

    @pl.loop(0, D // 128)
    def _(i):
        rows = pl.ds(pl.multiple_of(i * 128, 128), 128)
        both = dot(part, w_pairs[rows].reshape(256, WIDTH))
        w_split[0, rows, :] = both[:128].astype(BF16)
        w_split[1, rows, :] = both[128:].astype(BF16)

    row, col = iota((256, 256), 0), iota((256, 256), 1)
    reorder = onehot(col == (row & 7) * 32 + (row >> 4) * 2 + ((row >> 3) & 1))

    @pl.loop(1, Z)
    def _(k):
        come_a(k).wait_recv()

    out_b[...] = dot(reorder, in_a[...].reshape(256, 128)).astype(BF16).reshape(XY // 2, 32, 128)

    def send_b(k):
        return remote(
            out_b.at[lax.div(plane_peer(k), 2)], in_b.at[xy], ssem_b.at[k], rsem_b.at[xy],
            plane_id(k),
        )

    def come_b(k):
        at = plane_peer(k)
        return remote(
            out_b.at[lax.div(at, 2)], in_b.at[at], ssem_b.at[k], rsem_b.at[at], plane_id(k)
        )

    @pl.loop(1, XY)
    def _(k):
        send_b(k).start()

    in_b[xy] = out_b[lax.div(xy, 2)]

    slot = slot_tab[...]
    target = group_of(slot)
    placed = slot - target * TILES
    row = iota((512, 1), 0)
    bit = lax.rem(group, 2)
    pick = onehot(
        iota((512, Z * XY), 1) == ((row >> 5) & 3) * 32 + (row & 7) * 4 + (row >> 7)
    )
    goal = dot(pick, target.astype(F32).astype(BF16))
    place = dot(pick, placed.astype(F32).astype(BF16))
    matched = jnp.where(goal == (group - bit + ((row >> 4) & 1)).astype(F32), 1.0, 0.0)
    before = onehot(iota((TILES, TILES), 0) < iota((TILES, TILES), 1))
    rank = dot(matched.astype(BF16), before)
    brought = jnp.where(
        (matched > 0.5) & (rank == ((row >> 3) & 1).astype(F32)), place + 1.0, 0.0
    )
    landing[...] = brought.reshape(XY, 2, 16, TILES)
    spot_row = lax.dot_general(
        jnp.ones((8, TILES), BF16), brought.astype(BF16), NT, preferred_element_type=F32
    )[:1]
    hit = iota((TILES, 512), 0).astype(F32) + 1.0 == spot_row
    member = (iota((TILES, 512), 1) >> 4) & 1
    settle = jnp.concatenate([onehot(hit & (member == bit)), onehot(hit & (member != bit))], axis=0)

    text_load.wait()
    gain_load.wait()
    gain[...] = jnp.concatenate([gain_half[...], gain_half[...]], axis=1)
    text[...] = text_pairs[...].reshape(2 * TEXT_PAD, D)
    text_row, text_col = (iota((2 * TEXT_PAD, 2 * TEXT_PAD), i) for i in range(2))
    branch = jnp.where(text_row >= TEXT_PAD, 1, 0)
    part_text = onehot(text_col == (text_row - branch * TEXT_PAD) * 2 + branch)

    def project_text(c, out):
        projected = dot(text[...], w_split[c])
        if c == 0:
            slabs = [
                head_norm(projected[:, i * 128:(i + 1) * 128], gain[2:3, :]) for i in range(SLABS)
            ]
            projected = jnp.concatenate(slabs, axis=1)
        out[...] = dot(part_text, projected.astype(BF16)).astype(BF16).reshape(2, TEXT_PAD, WIDTH)

    project_text(0, tk)

    @pl.loop(1, XY)
    def _(k):
        come_b(k).wait_recv()

    tok[core] = dot(settle, in_b[...].reshape(512, 128)).astype(BF16).reshape(2, TILES, 128)

    send_c = remote(tok.at[core], tok.at[core], ssem_c, rsem_c, sibling_id)
    come_c = remote(tok.at[core], tok.at[other], ssem_c, rsem_c, sibling_id)
    send_c.start()

    project_text(1, tv)
    spot_column = jnp.sum(landing[:, bit].reshape(256, TILES), axis=1, keepdims=True)
    unsettle = onehot(spot_column == iota((256, TILES), 1).astype(F32) + 1.0)
    text_used = iota((TEXT_PAD, 128), 0) < TEXT
    for b in range(2):
        for s in range(SLABS):
            lanes = slice(s * 128, (s + 1) * 128)
            first = jnp.broadcast_to(tk[b, 0:1, lanes], (TEXT_PAD, 128))
            kbuf[b, s, 2 * ROWS:, :] = jnp.where(text_used, tk[b, :, lanes], first)
            vbuf[b, s, 2 * ROWS:, :128] = tv[b, :, lanes]
            vbuf[b, s, 2 * ROWS:, 128:] = onehot(text_used)

    own_len = live_ref[group]
    mate_len = jnp.where(partner_ref[group] != group, live_ref[mate], 0)
    row = iota((ROWS, 128), 0)
    quarter = sum(jnp.where(row >= TILES * j, 1, 0) for j in range(1, TILE))
    position = (row - quarter * TILES) * TILE + quarter

    for load in (mod_load, wemb_load, q_load, k_load, v_load):
        load.wait()
    come_c.wait_recv()
    mod_copy.wait_recv()

    for side in range(2):
        for j in range(TILE):
            line[side, j * TILES:(j + 1) * TILES, :] = (
                tok[j // 2, side][:, (j % 2) * CH:(j % 2 + 1) * CH]
            )

    def embed(side):
        for start in range(0, D, 256):
            lanes = slice(start, min(start + 256, D))
            hid[side, :, lanes] = dot(line[side], wemb[:, lanes])

    def norm(side, half, source):
        for i in range(2):
            rows = pl.ds(pl.multiple_of(half * HALF + i * TILES, 32), TILES)
            hidden = hid[side, rows, :]
            centred = hidden - jnp.mean(hidden, axis=-1, keepdims=True)
            spread = jnp.mean(centred * centred, axis=-1, keepdims=True)
            scaled = centred * lax.rsqrt(spread + EPS)
            for b in range(2):
                normed[2 * side + b, rows, :] = (
                    scaled * (1.0 + source[1, b:b + 1, :]) + source[0, b:b + 1, :]
                ).astype(BF16)

    def put(side, b, slab_index, slab):
        usable = position < (own_len if side == 0 else mate_len)
        rows = slice(side * ROWS, (side + 1) * ROWS)
        c, s = divmod(slab_index, SLABS)
        if c == 0:
            qbuf[b, s] = head_norm(slab, gain[0:1, :]).astype(BF16)
        elif c == 1:
            key = head_norm(slab, gain[1:2, :]).astype(BF16)
            first = jnp.broadcast_to(tk[b, 0:1, s * 128:(s + 1) * 128], key.shape)
            kbuf[b, s, rows, :] = jnp.where(usable, key, first)
        else:
            vbuf[b, s, rows, :128] = jnp.where(usable, slab, 0.0).astype(BF16)
            vbuf[b, s, rows, 128:] = onehot(usable)

    def project(side, b, slabs):
        for i in range(0, len(slabs), 2):
            pair = slabs[i:i + 2]
            out = dot(normed[2 * side + b], wqkv[:, pair[0] * 128:(pair[-1] + 1) * 128])
            for t, slab_index in enumerate(pair):
                put(side, b, slab_index, out[:, t * 128:(t + 1) * 128])

    embed(0)
    embed(1)

    @pl.loop(0, 2)
    def _(half):
        norm(0, half, mod)

    @pl.loop(0, 2)
    def _(b):
        project(0, b, list(range(3 * SLABS)))
        norm(1, b, mod_mate)

    @pl.loop(0, 2)
    def _(b):
        project(1, b, list(range(SLABS, 3 * SLABS)))

    def half_rows(b):
        return slice(b * HALF, (b + 1) * HALF) if isinstance(b, int) else pl.ds(
            pl.multiple_of(b * HALF, HALF), HALF
        )

    def exchange(b):
        return remote(
            normed.at[0, half_rows(b)], got.at[b], xsend.at[b], xrecv.at[b], sibling_id
        )

    def project_out(b, half, into):
        rows = att[b, pl.ds(pl.multiple_of(half * HALF, HALF), HALF), :]
        for start, size in CHUNKS:
            normed[into, half_rows(b), start:start + size] = dot(
                rows, wout[:, start:start + size]
            ).astype(BF16)

    lower = iota((HALF, 128), 1) < HEAD
    wout_load.wait()
    wfin_load.wait()

    def attend(b, half):
        rows = pl.ds(pl.multiple_of(half * HALF, HALF), HALF)
        for s in range(SLABS):
            query, key, value = qbuf[b, s, rows, :], kbuf[b, s], vbuf[b, s]
            parts = []
            for head in (lower, ~lower):
                scores = lax.dot_general(
                    jnp.where(head, query, jnp.zeros_like(query)), key, NT,
                    preferred_element_type=F32,
                )
                highest = jnp.max(scores, axis=-1, keepdims=True)
                raised = jnp.exp2((scores - highest) * (HEAD ** (-0.5) * LOG2E)).astype(BF16)
                both = dot(raised, value)
                parts.append(both[:, :128] / both[:, 128:])
            att[b, rows, s * 128:(s + 1) * 128] = jnp.where(lower, parts[0], parts[1]).astype(BF16)

    @pl.loop(0, 2)
    def _(b):
        attend(b, other)
        project_out(b, other, 0)
        exchange(b).start()

    @pl.loop(0, 2)
    def _(b):
        attend(b, core)
        project_out(b, core, 1)

    block = 48
    for b in range(2):
        exchange(b).wait_recv()
        gate, shift, scale = (mod[i, b:b + 1, :] for i in (2, 3, 4))

        @pl.loop(0, HALF // block)
        def _(i):
            rows = pl.ds(pl.multiple_of(i * block, block), block)
            kept = normed[1, pl.ds(pl.multiple_of(b * HALF + i * block, block), block), :]
            mixed = kept.astype(F32) + got[b, rows, :].astype(F32)
            mine = pl.ds(pl.multiple_of(core * HALF + i * block, block), block)
            state = hid[0, mine, :] + gate * mixed
            centred = state - jnp.mean(state, axis=-1, keepdims=True)
            spread = jnp.mean(centred * centred, axis=-1, keepdims=True)
            final = (centred * lax.rsqrt(spread + EPS) * (1.0 + scale) + shift).astype(BF16)
            vel[b, rows, :] = lax.dot_general(final, wfin[...], NT, preferred_element_type=F32)

    guided = vel[1] + GUIDE * (vel[0] - vel[1])
    row = iota((HALF, CH), 0)
    upper = jnp.where(row >= TILES, 1, 0)
    position = (row - upper * TILES) * TILE + 2 * core + upper
    change = jnp.where(position < own_len, STEP * guided, 0.0)
    change = jnp.concatenate([change[:TILES], change[TILES:]], axis=1).astype(BF16)
    home_b[...] = dot(unsettle, change).astype(BF16).reshape(XY, 16, 128)

    def return_b(k):
        return remote(
            home_b.at[plane_peer(k)], back_b.at[xy], hsend_b.at[k], hrecv_b.at[xy], plane_id(k)
        )

    def arrive_b(k):
        at = plane_peer(k)
        return remote(home_b.at[at], back_b.at[at], hsend_b.at[k], hrecv_b.at[at], plane_id(k))

    @pl.loop(1, XY)
    def _(k):
        return_b(k).start()

    back_b[xy] = home_b[xy]
    row, col = iota((256, 256), 0), iota((256, 256), 1)
    reorder = onehot(col == ((row >> 1) & 15) * 16 + (row & 1) * 8 + (row >> 5))
    collect = onehot(iota((TILES, 256), 1).astype(F32) == bucket_column)

    @pl.loop(1, XY)
    def _(k):
        arrive_b(k).wait_recv()

    home_a[...] = dot(reorder, back_b[...].reshape(256, 128)).astype(BF16).reshape(Z, 32, 128)

    def return_a(k):
        return remote(
            home_a.at[z_peer(k)], back_a.at[z], hsend_a.at[k], hrecv_a.at[z], z_id(k)
        )

    def arrive_a(k):
        at = z_peer(k)
        return remote(home_a.at[at], back_a.at[at], hsend_a.at[k], hrecv_a.at[at], z_id(k))

    @pl.loop(1, Z)
    def _(k):
        return_a(k).start()

    back_a[z] = home_a[z]

    @pl.loop(1, Z)
    def _(k):
        send_a(k).wait_send()

    @pl.loop(1, XY)
    def _(k):
        send_b(k).wait_send()
        return_b(k).wait_send()

    send_c.wait_send()
    mod_copy.wait_send()
    for b in range(2):
        exchange(b).wait_send()

    @pl.loop(1, Z)
    def _(k):
        arrive_a(k).wait_recv()

    out_ref[...] = lat[...] + dot(collect, back_a[...].reshape(256, 128))

    @pl.loop(1, Z)
    def _(k):
        return_a(k).wait_send()


def step(*operands):
    hbm = pl.BlockSpec(memory_space=pltpu.HBM)
    smem = pl.BlockSpec(memory_space=pltpu.SMEM)
    narrow, wide = pltpu.VMEM((Z, 32, 128), BF16), pltpu.VMEM((XY, 16, 128), BF16)
    dma = pltpu.SemaphoreType.DMA
    return pl.pallas_call(
        step_kernel,
        out_shape=jax.ShapeDtypeStruct((TILES, 128), F32),
        in_specs=[hbm] * 10 + [smem] * 2,
        out_specs=pl.BlockSpec(memory_space=pltpu.VMEM),
        scratch_shapes=[
            pltpu.VMEM((TILES, 128), F32),
            pltpu.VMEM((TILES, 128), jnp.int32),
            pltpu.VMEM((Z * XY, TILES), jnp.int32),
            pltpu.VMEM((5, 2, D), F32),
            pltpu.VMEM((2, 2, D), F32),
            pltpu.VMEM((3, HEAD), F32),
            pltpu.VMEM((3, 128), F32),
            pltpu.VMEM((TEXT_PAD, 2, D), BF16),
            pltpu.VMEM((2 * TEXT_PAD, D), BF16),
            pltpu.VMEM((D, 2, WIDTH), BF16),
            pltpu.VMEM((2, D, WIDTH), BF16),
            pltpu.VMEM((CH, D), BF16),
            pltpu.VMEM((D, 3 * WIDTH), BF16),
            pltpu.VMEM((WIDTH, D), BF16),
            pltpu.VMEM((CH, D), BF16),
            pltpu.VMEM((2, TEXT_PAD, WIDTH), BF16),
            pltpu.VMEM((2, TEXT_PAD, WIDTH), BF16),
            pltpu.VMEM((2, 2, TILES, 128), BF16),
            pltpu.VMEM((4, ROWS, D), BF16),
            pltpu.VMEM((2, SLABS, ROWS, 128), BF16),
            pltpu.VMEM((2, SLABS, KEYS, 128), BF16),
            pltpu.VMEM((2, SLABS, KEYS, 256), BF16),
            pltpu.VMEM((2, ROWS, WIDTH), BF16),
            pltpu.VMEM((2, HALF, D), BF16),
            pltpu.VMEM((2, ROWS, D), F32),
            pltpu.VMEM((2, ROWS, CH), BF16),
            pltpu.VMEM((2, HALF, CH), F32),
            pltpu.VMEM((XY, 2, 16, TILES), F32),
            narrow, narrow, narrow, pltpu.VMEM((XY, 32, 128), BF16), wide, wide, narrow, narrow,
            dma((12,)), dma((2,)), dma((Z,)), dma((Z,)), dma((XY,)), dma((XY,)),
            dma, dma, dma((2,)), dma((2,)),
            dma((XY,)), dma((XY,)), dma((Z,)), dma((Z,)),
        ],
        compiler_params=pltpu.CompilerParams(
            collective_id=0, has_side_effects=True, vmem_limit_bytes=62 << 20
        ),
        name="step",
    )(*operands)


def shards(
    latents, tile_slot, live, partner, text_states, modulation,
    w_embed, w_qkv, w_text_kv, w_out, w_final, norm_gains,
):
    return step(
        latents, tile_slot.reshape(TILES, 128), modulation[0].transpose(1, 0, 2),
        norm_gains, text_states[0].transpose(1, 0, 2),
        w_text_kv, w_embed, w_qkv.transpose(1, 0, 2), w_out, w_final.T, live, partner,
    )


def solution(mesh):
    placed = (
        P("groups", "mp"), P(), P(), P(),
        P("groups", None, None, None), P("groups", None, None, None),
        P(), P(None, None, "mp"), P(None, None, "mp"), P("mp", None), P(), P(),
    )
    return jax.shard_map(
        shards, mesh=mesh, in_specs=placed, out_specs=P("groups", "mp"), check_vma=False
    )
```

```python
import functools
import jax
import jax.numpy as jnp
from jax import lax
from jax.experimental import pallas as pl
from jax.experimental.pallas import tpu as pltpu
from jax.sharding import PartitionSpec as P

HEAD = 64
CH = 64
TEXT = 154
TEXT_PAD = 160
ROWS = 384
HALF = ROWS // 2
TILE = 4
TILES = 96
D = 2432
Z = 8
XY = 16
KEYS = 2 * ROWS + TEXT_PAD
WIDTH = 640
SLABS = WIDTH // 128
CHUNKS = ((0, 512), (512, 512), (1024, 512), (1536, 512), (2048, 384))

GUIDE = 3.5
STEP = -0.25
EPS = 1e-06
LOG2E = 1.4426950408889634
F32 = jnp.float32
BF16 = jnp.bfloat16
MESH = pl.DeviceIdType.MESH
NT = (((1,), (1,)), ((), ()))


def iota(shape, axis):
    return lax.broadcasted_iota(jnp.int32, shape, axis)


def onehot(condition):
    return jnp.where(condition, 1.0, 0.0).astype(BF16)


def dot(left, right):
    return jnp.dot(left, right, preferred_element_type=F32)


def group_of(slot):
    return (slot * 43691) >> 22


def head_norm(slab, gains):
    square = slab * slab
    lower = iota(slab.shape, 1) < HEAD
    first = jnp.sum(jnp.where(lower, square, 0.0), axis=-1, keepdims=True) * (1.0 / HEAD)
    second = jnp.sum(jnp.where(lower, 0.0, square), axis=-1, keepdims=True) * (1.0 / HEAD)
    return slab * jnp.where(lower, lax.rsqrt(first + EPS), lax.rsqrt(second + EPS)) * gains


def step_kernel(
    lat_hbm, slot_hbm, mod_hbm, gain_hbm, text_hbm, wtext_hbm, wemb_hbm, wqkv_hbm, wout_hbm,
    wfin_hbm, live_ref, partner_ref, out_ref,
    lat, slot_raw, slot_tab, mod, mod_mate, gain_half, gain, text_pairs, w_pairs, w_split, wemb, wqkv,
    wout, wfin, tk, tv, tok, normed, qbuf, kbuf, vbuf, att, got, hid, line, vel, landing,
    out_a, in_a, out_b, in_b, home_b, back_b, home_a, back_a,
    lsem, msem, ssem_a, rsem_a, ssem_b, rsem_b, ssem_c, rsem_c, xsend, xrecv,
    hsend_b, hrecv_b, hsend_a, hrecv_a,
):
    group, core = lax.axis_index("groups"), lax.axis_index("mp")
    z, xy = lax.div(group, XY), lax.rem(group, XY)
    other = 1 - core
    mate = group + 1 - 2 * lax.rem(group, 2)
    sibling_id = {"groups": group, "mp": other}
    mate_id = {"groups": mate, "mp": core}

    def z_peer(k):
        return lax.rem(z + k, Z)

    def z_id(k):
        return {"groups": z_peer(k) * XY + xy, "mp": core}

    def plane_peer(k):
        return lax.rem(xy + k, XY)

    def plane_id(k):
        return {"groups": z * XY + plane_peer(k), "mp": core}

    def remote(src, dst, send, recv, to):
        return pltpu.make_async_remote_copy(
            src_ref=src, dst_ref=dst, send_sem=send, recv_sem=recv,
            device_id=to, device_id_type=MESH,
        )

    barrier = pltpu.get_barrier_semaphore()

    @pl.loop(1, Z)
    def _(k):
        pl.semaphore_signal(barrier, inc=1, device_id=z_id(k), device_id_type=MESH)

    @pl.loop(1, XY)
    def _(k):
        pl.semaphore_signal(barrier, inc=1, device_id=plane_id(k), device_id_type=MESH)

    pl.semaphore_signal(barrier, inc=1, device_id=sibling_id, device_id_type=MESH)

    loads = [
        (slot_hbm, slot_raw), (lat_hbm, lat), (text_hbm, text_pairs.at[pl.ds(0, TEXT)]),
        (wtext_hbm, w_pairs), (gain_hbm, gain_half), (mod_hbm, mod), (wemb_hbm, wemb),
    ] + [
        (wqkv_hbm.at[c], wqkv.at[:, pl.ds(c * WIDTH, WIDTH)]) for c in range(3)
    ] + [(wout_hbm, wout), (wfin_hbm, wfin)]
    loads = [
        pltpu.make_async_copy(src, dst, lsem.at[i]) for i, (src, dst) in enumerate(loads)
    ]
    (slot_load, lat_load, text_load, wtext_load, gain_load, mod_load, wemb_load,
     q_load, k_load, v_load, wout_load, wfin_load) = loads
    for load in loads:
        load.start()
    text_pairs[TEXT:] = jnp.zeros((TEXT_PAD - TEXT, 2, D), BF16)

    slot_load.wait()
    three = jnp.concatenate([slot_raw[pl.ds(i, 32, stride=3), :] for i in range(3)], axis=1)
    for k in range(4):
        slot_tab[32 * k:32 * (k + 1), :] = three[:, TILES * k:TILES * (k + 1)]

    mine = slot_tab[pl.ds(lax.rem(group, 4) * 32 + lax.div(group, 4), 1), :]
    mine = jnp.broadcast_to(group_of(mine).astype(F32), (TILES, TILES))
    across, down = iota((TILES, TILES), 1), iota((TILES, TILES), 0)
    column = jnp.sum(jnp.where(across == down, mine, 0.0), axis=1, keepdims=True)
    same = mine == column
    bucket_row = 2.0 * mine[:1] + jnp.sum(
        jnp.where(same & (down < across), 1.0, 0.0), axis=0, keepdims=True
    )
    bucket_column = 2.0 * column + jnp.sum(
        jnp.where(same & (across < down), 1.0, 0.0), axis=1, keepdims=True
    )
    sender = onehot(iota((256, TILES), 0).astype(F32) == bucket_row)
    lat_load.wait()
    out_a[...] = dot(sender, lat[...].astype(BF16)).astype(BF16).reshape(Z, 32, 128)

    pl.semaphore_wait(barrier, Z - 1 + XY - 1 + 1)

    def send_a(k):
        return remote(out_a.at[z_peer(k)], in_a.at[z], ssem_a.at[k], rsem_a.at[z], z_id(k))

    def come_a(k):
        at = z_peer(k)
        return remote(out_a.at[at], in_a.at[at], ssem_a.at[k], rsem_a.at[at], z_id(k))

    @pl.loop(1, Z)
    def _(k):
        send_a(k).start()

    mod_copy = remote(mod_hbm.at[pl.ds(0, 2)], mod_mate, msem.at[0], msem.at[1], mate_id)
    mod_copy.start()
    in_a[z] = out_a[z]

    part_row = iota((256, 256), 0)
    part = onehot(iota((256, 256), 1) == (part_row & 127) * 2 + (part_row >> 7))
    wtext_load.wait()

    @pl.loop(0, D // 128)
    def _(i):
        rows = pl.ds(pl.multiple_of(i * 128, 128), 128)
        both = dot(part, w_pairs[rows].reshape(256, WIDTH))
        w_split[0, rows, :] = both[:128].astype(BF16)
        w_split[1, rows, :] = both[128:].astype(BF16)

    slot = slot_tab[...]
    target = group_of(slot)
    placed = slot - target * TILES
    row = iota((512, 1), 0)
    bit = lax.rem(group, 2)
    pick = onehot(
        iota((512, Z * XY), 1) == ((row >> 5) & 3) * 32 + (row & 7) * 4 + (row >> 7)
    )
    goal = dot(pick, target.astype(F32).astype(BF16))
    place = dot(pick, placed.astype(F32).astype(BF16))
    matched = jnp.where(goal == (group - bit + ((row >> 4) & 1)).astype(F32), 1.0, 0.0)
    before = onehot(iota((TILES, TILES), 0) < iota((TILES, TILES), 1))
    rank = dot(matched.astype(BF16), before)
    brought = jnp.where(
        (matched > 0.5) & (rank == ((row >> 3) & 1).astype(F32)), place + 1.0, 0.0
    )
    landing[...] = brought.reshape(XY, 2, 16, TILES)
    spot_row = lax.dot_general(
        jnp.ones((8, TILES), BF16), brought.astype(BF16), NT, preferred_element_type=F32
    )[:1]
    hit = iota((TILES, 512), 0).astype(F32) + 1.0 == spot_row
    member = (iota((TILES, 512), 1) >> 4) & 1
    spot_column = jnp.sum(landing[:, bit].reshape(256, TILES), axis=1, keepdims=True)
    unsettle = onehot(spot_column == iota((256, TILES), 1).astype(F32) + 1.0)
    settle = jnp.concatenate([onehot(hit & (member == bit)), onehot(hit & (member != bit))], axis=0)

    row, col = iota((256, 256), 0), iota((256, 256), 1)
    reorder = onehot(col == (row & 7) * 32 + (row >> 4) * 2 + ((row >> 3) & 1))

    @pl.loop(1, Z)
    def _(k):
        come_a(k).wait_recv()

    out_b[...] = dot(reorder, in_a[...].reshape(256, 128)).astype(BF16).reshape(XY // 2, 32, 128)

    def send_b(k):
        return remote(
            out_b.at[lax.div(plane_peer(k), 2)], in_b.at[xy], ssem_b.at[k], rsem_b.at[xy],
            plane_id(k),
        )

    def come_b(k):
        at = plane_peer(k)
        return remote(
            out_b.at[lax.div(at, 2)], in_b.at[at], ssem_b.at[k], rsem_b.at[at], plane_id(k)
        )

    @pl.loop(1, XY)
    def _(k):
        send_b(k).start()

    in_b[xy] = out_b[lax.div(xy, 2)]

    text_load.wait()
    gain_load.wait()
    gain[...] = jnp.concatenate([gain_half[...], gain_half[...]], axis=1)
    text_row, text_col = (iota((2 * TEXT_PAD, 2 * TEXT_PAD), i) for i in range(2))
    branch = jnp.where(text_row >= TEXT_PAD, 1, 0)
    part_text = onehot(text_col == (text_row - branch * TEXT_PAD) * 2 + branch)

    def project_text(c, out):
        projected = dot(text_pairs[...].reshape(2 * TEXT_PAD, D), w_split[c])
        if c == 0:
            slabs = [
                head_norm(projected[:, i * 128:(i + 1) * 128], gain[2:3, :]) for i in range(SLABS)
            ]
            projected = jnp.concatenate(slabs, axis=1)
        out[...] = dot(part_text, projected.astype(BF16)).astype(BF16).reshape(2, TEXT_PAD, WIDTH)

    project_text(0, tk)
    project_text(1, tv)
    text_used = iota((TEXT_PAD, 128), 0) < TEXT
    for b in range(2):
        for s in range(SLABS):
            lanes = slice(s * 128, (s + 1) * 128)
            first = jnp.broadcast_to(tk[b, 0:1, lanes], (TEXT_PAD, 128))
            kbuf[b, s, 2 * ROWS:, :] = jnp.where(text_used, tk[b, :, lanes], first)
            vbuf[b, s, 2 * ROWS:, :128] = tv[b, :, lanes]
            vbuf[b, s, 2 * ROWS:, 128:] = onehot(text_used)


    @pl.loop(1, XY)
    def _(k):
        come_b(k).wait_recv()

    tok[core] = dot(settle, in_b[...].reshape(512, 128)).astype(BF16).reshape(2, TILES, 128)

    send_c = remote(tok.at[core], tok.at[core], ssem_c, rsem_c, sibling_id)
    come_c = remote(tok.at[core], tok.at[other], ssem_c, rsem_c, sibling_id)
    send_c.start()

    own_len = live_ref[group]
    mate_len = jnp.where(partner_ref[group] != group, live_ref[mate], 0)
    row = iota((ROWS, 128), 0)
    quarter = sum(jnp.where(row >= TILES * j, 1, 0) for j in range(1, TILE))
    position = (row - quarter * TILES) * TILE + quarter

    for load in (mod_load, wemb_load, q_load, k_load, v_load):
        load.wait()
    come_c.wait_recv()
    mod_copy.wait_recv()

    for side in range(2):
        for j in range(TILE):
            line[side, j * TILES:(j + 1) * TILES, :] = (
                tok[j // 2, side][:, (j % 2) * CH:(j % 2 + 1) * CH]
            )

    def embed(side):
        for start in range(0, D, 256):
            lanes = slice(start, min(start + 256, D))
            hid[side, :, lanes] = dot(line[side], wemb[:, lanes])

    def norm(side, half, source):
        for i in range(2):
            rows = pl.ds(half * HALF + i * TILES if isinstance(half, int) else pl.multiple_of(half * HALF + i * TILES, 32), TILES)
            hidden = hid[side, rows, :]
            centred = hidden - jnp.mean(hidden, axis=-1, keepdims=True)
            spread = jnp.mean(centred * centred, axis=-1, keepdims=True)
            scaled = centred * lax.rsqrt(spread + EPS)
            for b in range(2):
                normed[2 * side + b, rows, :] = (
                    scaled * (1.0 + source[1, b:b + 1, :]) + source[0, b:b + 1, :]
                ).astype(BF16)

    def put(side, b, slab_index, slab):
        usable = position < (own_len if side == 0 else mate_len)
        rows = slice(side * ROWS, (side + 1) * ROWS)
        c, s = divmod(slab_index, SLABS)
        if c == 0:
            qbuf[b, s] = head_norm(slab, gain[0:1, :]).astype(BF16)
        elif c == 1:
            key = head_norm(slab, gain[1:2, :]).astype(BF16)
            first = jnp.broadcast_to(tk[b, 0:1, s * 128:(s + 1) * 128], key.shape)
            kbuf[b, s, rows, :] = jnp.where(usable, key, first)
        else:
            vbuf[b, s, rows, :128] = jnp.where(usable, slab, 0.0).astype(BF16)
            vbuf[b, s, rows, 128:] = onehot(usable)

    def project(side, b, slabs):
        for i in range(0, len(slabs), 2):
            pair = slabs[i:i + 2]
            out = dot(normed[2 * side + b], wqkv[:, pair[0] * 128:(pair[-1] + 1) * 128])
            for t, slab_index in enumerate(pair):
                put(side, b, slab_index, out[:, t * 128:(t + 1) * 128])

    embed(0)

    @pl.loop(0, 2)
    def _(half):
        norm(0, half, mod)

    embed(1)

    for b in range(2):
        norm(1, b, mod_mate)
        project(0, b, list(range(3 * SLABS)))

    for b in range(2):
        project(1, b, list(range(SLABS, 3 * SLABS)))

    def half_rows(b):
        return slice(b * HALF, (b + 1) * HALF) if isinstance(b, int) else pl.ds(
            pl.multiple_of(b * HALF, HALF), HALF
        )

    def exchange(b):
        return remote(
            normed.at[0, half_rows(b)], got.at[b], xsend.at[b], xrecv.at[b], sibling_id
        )

    def project_out(b, half, into):
        rows = att[b, pl.ds(pl.multiple_of(half * HALF, HALF), HALF), :]
        for start, size in CHUNKS:
            normed[into, half_rows(b), start:start + size] = dot(
                rows, wout[:, start:start + size]
            ).astype(BF16)

    lower = iota((ROWS, 128), 1) < HEAD
    wout_load.wait()
    wfin_load.wait()

    def attend(b):
        for s in range(SLABS):
            query, key, value = qbuf[b, s], kbuf[b, s], vbuf[b, s]
            parts = []
            for head in (lower, ~lower):
                scores = lax.dot_general(
                    jnp.where(head, query, jnp.zeros_like(query)), key, NT,
                    preferred_element_type=F32,
                )
                highest = jnp.max(scores, axis=-1, keepdims=True)
                raised = jnp.exp2((scores - highest) * (HEAD ** (-0.5) * LOG2E)).astype(BF16)
                both = dot(raised, value)
                parts.append(both[:, :128] / both[:, 128:])
            att[b, :, s * 128:(s + 1) * 128] = jnp.where(lower, parts[0], parts[1]).astype(BF16)

    @pl.loop(0, 2)
    def _(b):
        attend(b)
        project_out(b, other, 0)
        exchange(b).start()

    for b in range(2):
        project_out(b, core, 1)

    block = 48
    for b in range(2):
        exchange(b).wait_recv()
        gate, shift, scale = (mod[i, b:b + 1, :] for i in (2, 3, 4))

        @pl.loop(0, HALF // block)
        def _(i):
            rows = pl.ds(pl.multiple_of(i * block, block), block)
            kept = normed[1, pl.ds(pl.multiple_of(b * HALF + i * block, block), block), :]
            mixed = kept.astype(F32) + got[b, rows, :].astype(F32)
            mine = pl.ds(pl.multiple_of(core * HALF + i * block, block), block)
            state = hid[0, mine, :] + gate * mixed
            centred = state - jnp.mean(state, axis=-1, keepdims=True)
            spread = jnp.mean(centred * centred, axis=-1, keepdims=True)
            final = (centred * lax.rsqrt(spread + EPS) * (1.0 + scale) + shift).astype(BF16)
            vel[b, rows, :] = lax.dot_general(final, wfin[...], NT, preferred_element_type=F32)

    guided = vel[1] + GUIDE * (vel[0] - vel[1])
    row = iota((HALF, CH), 0)
    upper = jnp.where(row >= TILES, 1, 0)
    position = (row - upper * TILES) * TILE + 2 * core + upper
    change = jnp.where(position < own_len, STEP * guided, 0.0)
    change = jnp.concatenate([change[:TILES], change[TILES:]], axis=1).astype(BF16)
    home_b[...] = dot(unsettle, change).astype(BF16).reshape(XY, 16, 128)

    def return_b(k):
        return remote(
            home_b.at[plane_peer(k)], back_b.at[xy], hsend_b.at[k], hrecv_b.at[xy], plane_id(k)
        )

    def arrive_b(k):
        at = plane_peer(k)
        return remote(home_b.at[at], back_b.at[at], hsend_b.at[k], hrecv_b.at[at], plane_id(k))

    @pl.loop(1, XY)
    def _(k):
        return_b(k).start()

    back_b[xy] = home_b[xy]
    row, col = iota((256, 256), 0), iota((256, 256), 1)
    reorder = onehot(col == ((row >> 1) & 15) * 16 + (row & 1) * 8 + (row >> 5))
    collect = onehot(iota((TILES, 256), 1).astype(F32) == bucket_column)

    @pl.loop(1, XY)
    def _(k):
        arrive_b(k).wait_recv()

    home_a[...] = dot(reorder, back_b[...].reshape(256, 128)).astype(BF16).reshape(Z, 32, 128)

    def return_a(k):
        return remote(
            home_a.at[z_peer(k)], back_a.at[z], hsend_a.at[k], hrecv_a.at[z], z_id(k)
        )

    def arrive_a(k):
        at = z_peer(k)
        return remote(home_a.at[at], back_a.at[at], hsend_a.at[k], hrecv_a.at[at], z_id(k))

    @pl.loop(1, Z)
    def _(k):
        return_a(k).start()

    back_a[z] = home_a[z]

    @pl.loop(1, Z)
    def _(k):
        send_a(k).wait_send()

    @pl.loop(1, XY)
    def _(k):
        send_b(k).wait_send()
        return_b(k).wait_send()

    send_c.wait_send()
    mod_copy.wait_send()
    for b in range(2):
        exchange(b).wait_send()

    @pl.loop(1, Z)
    def _(k):
        arrive_a(k).wait_recv()

    out_ref[...] = lat[...] + dot(collect, back_a[...].reshape(256, 128))

    @pl.loop(1, Z)
    def _(k):
        return_a(k).wait_send()


def step(*operands):
    hbm = pl.BlockSpec(memory_space=pltpu.HBM)
    smem = pl.BlockSpec(memory_space=pltpu.SMEM)
    narrow, wide = pltpu.VMEM((Z, 32, 128), BF16), pltpu.VMEM((XY, 16, 128), BF16)
    dma = pltpu.SemaphoreType.DMA
    return pl.pallas_call(
        step_kernel,
        out_shape=jax.ShapeDtypeStruct((TILES, 128), F32),
        in_specs=[hbm] * 10 + [smem] * 2,
        out_specs=pl.BlockSpec(memory_space=pltpu.VMEM),
        scratch_shapes=[
            pltpu.VMEM((TILES, 128), F32),
            pltpu.VMEM((TILES, 128), jnp.int32),
            pltpu.VMEM((Z * XY, TILES), jnp.int32),
            pltpu.VMEM((5, 2, D), F32),
            pltpu.VMEM((2, 2, D), F32),
            pltpu.VMEM((3, HEAD), F32),
            pltpu.VMEM((3, 128), F32),
            pltpu.VMEM((TEXT_PAD, 2, D), BF16),
            pltpu.VMEM((D, 2, WIDTH), BF16),
            pltpu.VMEM((2, D, WIDTH), BF16),
            pltpu.VMEM((CH, D), BF16),
            pltpu.VMEM((D, 3 * WIDTH), BF16),
            pltpu.VMEM((WIDTH, D), BF16),
            pltpu.VMEM((CH, D), BF16),
            pltpu.VMEM((2, TEXT_PAD, WIDTH), BF16),
            pltpu.VMEM((2, TEXT_PAD, WIDTH), BF16),
            pltpu.VMEM((2, 2, TILES, 128), BF16),
            pltpu.VMEM((4, ROWS, D), BF16),
            pltpu.VMEM((2, SLABS, ROWS, 128), BF16),
            pltpu.VMEM((2, SLABS, KEYS, 128), BF16),
            pltpu.VMEM((2, SLABS, KEYS, 256), BF16),
            pltpu.VMEM((2, ROWS, WIDTH), BF16),
            pltpu.VMEM((2, HALF, D), BF16),
            pltpu.VMEM((2, ROWS, D), F32),
            pltpu.VMEM((2, ROWS, CH), BF16),
            pltpu.VMEM((2, HALF, CH), F32),
            pltpu.VMEM((XY, 2, 16, TILES), F32),
            narrow, narrow, narrow, pltpu.VMEM((XY, 32, 128), BF16), wide, wide, narrow, narrow,
            dma((12,)), dma((2,)), dma((Z,)), dma((Z,)), dma((XY,)), dma((XY,)),
            dma, dma, dma((2,)), dma((2,)),
            dma((XY,)), dma((XY,)), dma((Z,)), dma((Z,)),
        ],
        compiler_params=pltpu.CompilerParams(
            collective_id=0, has_side_effects=True, vmem_limit_bytes=63 << 20
        ),
        name="step",
    )(*operands)


def shards(
    latents, tile_slot, live, partner, text_states, modulation,
    w_embed, w_qkv, w_text_kv, w_out, w_final, norm_gains,
):
    return step(
        latents, tile_slot.reshape(TILES, 128), modulation[0].transpose(1, 0, 2),
        norm_gains, text_states[0].transpose(1, 0, 2),
        w_text_kv, w_embed, w_qkv.transpose(1, 0, 2), w_out, w_final.T, live, partner,
    )


def solution(mesh):
    placed = (
        P("groups", "mp"), P(), P(), P(),
        P("groups", None, None, None), P("groups", None, None, None),
        P(), P(None, None, "mp"), P(None, None, "mp"), P("mp", None), P(), P(),
    )
    return jax.shard_map(
        shards, mesh=mesh, in_specs=placed, out_specs=P("groups", "mp"), check_vma=False
    )
```

```python
import functools
import jax
import jax.numpy as jnp
from jax import lax
from jax.experimental import pallas as pl
from jax.experimental.pallas import tpu as pltpu
from jax.sharding import PartitionSpec as P

HEAD = 64
CH = 64
TEXT = 154
TEXT_PAD = 160
ROWS = 384
HALF = ROWS // 2
TILE = 4
TILES = 96
D = 2432
Z = 8
XY = 16
KEYS = 2 * ROWS + TEXT_PAD
WIDTH = 640
SLABS = WIDTH // 128
CHUNKS = ((0, 512), (512, 512), (1024, 512), (1536, 512), (2048, 384))

GUIDE = 3.5
STEP = -0.25
EPS = 1e-06
LOG2E = 1.4426950408889634
F32 = jnp.float32
BF16 = jnp.bfloat16
MESH = pl.DeviceIdType.MESH
NT = (((1,), (1,)), ((), ()))


def iota(shape, axis):
    return lax.broadcasted_iota(jnp.int32, shape, axis)


def onehot(condition):
    return jnp.where(condition, 1.0, 0.0).astype(BF16)


def dot(left, right):
    return jnp.dot(left, right, preferred_element_type=F32)


def group_of(slot):
    return (slot * 43691) >> 22


def head_norm(slab, gains):
    square = slab * slab
    lower = iota(slab.shape, 1) < HEAD
    first = jnp.sum(jnp.where(lower, square, 0.0), axis=-1, keepdims=True) * (1.0 / HEAD)
    second = jnp.sum(jnp.where(lower, 0.0, square), axis=-1, keepdims=True) * (1.0 / HEAD)
    return slab * jnp.where(lower, lax.rsqrt(first + EPS), lax.rsqrt(second + EPS)) * gains


def step_kernel(
    lat_hbm, slot_hbm, mod_hbm, gain_hbm, text_hbm, wtext_hbm, wemb_hbm, wqkv_hbm, wout_hbm,
    wfin_hbm, live_ref, partner_ref, out_ref,
    lat, slot_raw, slot_tab, mod, mod_mate, gain_half, gain, text_pairs, w_pairs, w_split, wemb, wqkv,
    wout, wfin, tk, tv, tok, normed, qbuf, kbuf, vbuf, att, got, hid, line, landing,
    out_a, in_a, out_b, in_b, home_b, back_b, home_a, back_a,
    lsem, msem, ssem_a, rsem_a, ssem_b, rsem_b, ssem_c, rsem_c, xsend, xrecv,
    hsend_b, hrecv_b, hsend_a, hrecv_a,
):
    group, core = lax.axis_index("groups"), lax.axis_index("mp")
    z, xy = lax.div(group, XY), lax.rem(group, XY)
    other = 1 - core
    mate = group + 1 - 2 * lax.rem(group, 2)
    sibling_id = {"groups": group, "mp": other}
    mate_id = {"groups": mate, "mp": core}

    def z_peer(k):
        return lax.rem(z + k, Z)

    def z_id(k):
        return {"groups": z_peer(k) * XY + xy, "mp": core}

    def plane_peer(k):
        return lax.rem(xy + k, XY)

    def plane_id(k):
        return {"groups": z * XY + plane_peer(k), "mp": core}

    def remote(src, dst, send, recv, to):
        return pltpu.make_async_remote_copy(
            src_ref=src, dst_ref=dst, send_sem=send, recv_sem=recv,
            device_id=to, device_id_type=MESH,
        )

    barrier = pltpu.get_barrier_semaphore()

    @pl.loop(1, Z)
    def _(k):
        pl.semaphore_signal(barrier, inc=1, device_id=z_id(k), device_id_type=MESH)

    @pl.loop(1, XY)
    def _(k):
        pl.semaphore_signal(barrier, inc=1, device_id=plane_id(k), device_id_type=MESH)

    pl.semaphore_signal(barrier, inc=1, device_id=sibling_id, device_id_type=MESH)

    loads = [
        (slot_hbm, slot_raw), (lat_hbm, lat), (text_hbm, text_pairs.at[pl.ds(0, TEXT)]),
        (wtext_hbm, w_pairs), (gain_hbm, gain_half), (mod_hbm, mod), (wemb_hbm, wemb),
    ] + [
        (wqkv_hbm.at[c], wqkv.at[:, pl.ds(c * WIDTH, WIDTH)]) for c in range(3)
    ] + [(wout_hbm, wout), (wfin_hbm, wfin)]
    loads = [
        pltpu.make_async_copy(src, dst, lsem.at[i]) for i, (src, dst) in enumerate(loads)
    ]
    (slot_load, lat_load, text_load, wtext_load, gain_load, mod_load, wemb_load,
     q_load, k_load, v_load, wout_load, wfin_load) = loads
    for load in loads:
        load.start()
    text_pairs[TEXT:] = jnp.zeros((TEXT_PAD - TEXT, 2, D), BF16)

    slot_load.wait()
    three = jnp.concatenate([slot_raw[pl.ds(i, 32, stride=3), :] for i in range(3)], axis=1)
    for k in range(4):
        slot_tab[32 * k:32 * (k + 1), :] = three[:, TILES * k:TILES * (k + 1)]

    mine = slot_tab[pl.ds(lax.rem(group, 4) * 32 + lax.div(group, 4), 1), :]
    mine = jnp.broadcast_to(group_of(mine).astype(F32), (TILES, TILES))
    across, down = iota((TILES, TILES), 1), iota((TILES, TILES), 0)
    column = jnp.sum(jnp.where(across == down, mine, 0.0), axis=1, keepdims=True)
    same = mine == column
    bucket_row = 2.0 * mine[:1] + jnp.sum(
        jnp.where(same & (down < across), 1.0, 0.0), axis=0, keepdims=True
    )
    bucket_column = 2.0 * column + jnp.sum(
        jnp.where(same & (across < down), 1.0, 0.0), axis=1, keepdims=True
    )
    sender = onehot(iota((256, TILES), 0).astype(F32) == bucket_row)
    lat_load.wait()
    out_a[...] = dot(sender, lat[...].astype(BF16)).astype(BF16).reshape(Z, 32, 128)

    pl.semaphore_wait(barrier, Z - 1 + XY - 1 + 1)

    def send_a(k):
        return remote(out_a.at[z_peer(k)], in_a.at[z], ssem_a.at[k], rsem_a.at[z], z_id(k))

    def come_a(k):
        at = z_peer(k)
        return remote(out_a.at[at], in_a.at[at], ssem_a.at[k], rsem_a.at[at], z_id(k))

    @pl.loop(1, Z)
    def _(k):
        send_a(k).start()

    mod_copy = remote(mod_hbm.at[pl.ds(0, 2)], mod_mate, msem.at[0], msem.at[1], mate_id)
    mod_copy.start()
    in_a[z] = out_a[z]

    part_row = iota((256, 256), 0)
    part = onehot(iota((256, 256), 1) == (part_row & 127) * 2 + (part_row >> 7))
    wtext_load.wait()

    @pl.loop(0, D // 128)
    def _(i):
        rows = pl.ds(pl.multiple_of(i * 128, 128), 128)
        both = dot(part, w_pairs[rows].reshape(256, WIDTH))
        w_split[0, rows, :] = both[:128].astype(BF16)
        w_split[1, rows, :] = both[128:].astype(BF16)

    slot = slot_tab[...]
    target = group_of(slot)
    placed = slot - target * TILES
    row = iota((512, 1), 0)
    bit = lax.rem(group, 2)
    pick = onehot(
        iota((512, Z * XY), 1) == ((row >> 5) & 3) * 32 + (row & 7) * 4 + (row >> 7)
    )
    goal = dot(pick, target.astype(F32).astype(BF16))
    place = dot(pick, placed.astype(F32).astype(BF16))
    matched = jnp.where(goal == (group - bit + ((row >> 4) & 1)).astype(F32), 1.0, 0.0)
    before = onehot(iota((TILES, TILES), 0) < iota((TILES, TILES), 1))
    rank = dot(matched.astype(BF16), before)
    brought = jnp.where(
        (matched > 0.5) & (rank == ((row >> 3) & 1).astype(F32)), place + 1.0, 0.0
    )
    landing[...] = brought.reshape(XY, 2, 16, TILES)
    spot_row = lax.dot_general(
        jnp.ones((8, TILES), BF16), brought.astype(BF16), NT, preferred_element_type=F32
    )[:1]
    hit = iota((TILES, 512), 0).astype(F32) + 1.0 == spot_row
    member = (iota((TILES, 512), 1) >> 4) & 1
    spot_column = jnp.sum(landing[:, bit].reshape(256, TILES), axis=1, keepdims=True)
    unsettle = onehot(spot_column == iota((256, TILES), 1).astype(F32) + 1.0)
    settle = jnp.concatenate([onehot(hit & (member == bit)), onehot(hit & (member != bit))], axis=0)

    row, col = iota((256, 256), 0), iota((256, 256), 1)
    reorder = onehot(col == (row & 7) * 32 + (row >> 4) * 2 + ((row >> 3) & 1))

    @pl.loop(1, Z)
    def _(k):
        come_a(k).wait_recv()

    out_b[...] = dot(reorder, in_a[...].reshape(256, 128)).astype(BF16).reshape(XY // 2, 32, 128)

    def send_b(k):
        return remote(
            out_b.at[lax.div(plane_peer(k), 2)], in_b.at[xy], ssem_b.at[k], rsem_b.at[xy],
            plane_id(k),
        )

    def come_b(k):
        at = plane_peer(k)
        return remote(
            out_b.at[lax.div(at, 2)], in_b.at[at], ssem_b.at[k], rsem_b.at[at], plane_id(k)
        )

    @pl.loop(1, XY)
    def _(k):
        send_b(k).start()

    in_b[xy] = out_b[lax.div(xy, 2)]

    text_load.wait()
    gain_load.wait()
    gain[...] = jnp.concatenate([gain_half[...], gain_half[...]], axis=1)
    text_row, text_col = (iota((2 * TEXT_PAD, 2 * TEXT_PAD), i) for i in range(2))
    branch = jnp.where(text_row >= TEXT_PAD, 1, 0)
    part_text = onehot(text_col == (text_row - branch * TEXT_PAD) * 2 + branch)

    def project_text(c, out):
        projected = dot(text_pairs[...].reshape(2 * TEXT_PAD, D), w_split[c])
        if c == 0:
            slabs = [
                head_norm(projected[:, i * 128:(i + 1) * 128], gain[2:3, :]) for i in range(SLABS)
            ]
            projected = jnp.concatenate(slabs, axis=1)
        out[...] = dot(part_text, projected.astype(BF16)).astype(BF16).reshape(2, TEXT_PAD, WIDTH)

    project_text(0, tk)
    project_text(1, tv)
    text_used = iota((TEXT_PAD, 128), 0) < TEXT
    for b in range(2):
        for s in range(SLABS):
            lanes = slice(s * 128, (s + 1) * 128)
            first = jnp.broadcast_to(tk[b, 0:1, lanes], (TEXT_PAD, 128))
            kbuf[b, s, 2 * ROWS:, :] = jnp.where(text_used, tk[b, :, lanes], first)
            vbuf[b, s, 2 * ROWS:, :128] = tv[b, :, lanes]
            vbuf[b, s, 2 * ROWS:, 128:] = onehot(text_used)


    @pl.loop(1, XY)
    def _(k):
        come_b(k).wait_recv()

    tok[core] = dot(settle, in_b[...].reshape(512, 128)).astype(BF16).reshape(2, TILES, 128)

    send_c = remote(tok.at[core], tok.at[core], ssem_c, rsem_c, sibling_id)
    come_c = remote(tok.at[core], tok.at[other], ssem_c, rsem_c, sibling_id)
    send_c.start()

    own_len = live_ref[group]
    mate_len = jnp.where(partner_ref[group] != group, live_ref[mate], 0)
    row = iota((ROWS, 128), 0)
    quarter = sum(jnp.where(row >= TILES * j, 1, 0) for j in range(1, TILE))
    position = (row - quarter * TILES) * TILE + quarter

    for load in (mod_load, wemb_load, q_load, k_load, v_load):
        load.wait()
    come_c.wait_recv()
    mod_copy.wait_recv()

    for side in range(2):
        for j in range(TILE):
            line[side, j * TILES:(j + 1) * TILES, :] = (
                tok[j // 2, side][:, (j % 2) * CH:(j % 2 + 1) * CH]
            )

    def embed(side):
        for start in range(0, D, 256):
            lanes = slice(start, min(start + 256, D))
            hid[side, :, lanes] = dot(line[side], wemb[:, lanes])

    def norm(side, half, source):
        for i in range(2):
            rows = pl.ds(half * HALF + i * TILES if isinstance(half, int) else pl.multiple_of(half * HALF + i * TILES, 32), TILES)
            hidden = hid[side, rows, :]
            centred = hidden - jnp.mean(hidden, axis=-1, keepdims=True)
            spread = jnp.mean(centred * centred, axis=-1, keepdims=True)
            scaled = centred * lax.rsqrt(spread + EPS)
            for b in range(2):
                normed[2 * side + b, rows, :] = (
                    scaled * (1.0 + source[1, b:b + 1, :]) + source[0, b:b + 1, :]
                ).astype(BF16)

    def put(side, b, slab_index, slab):
        usable = position < (own_len if side == 0 else mate_len)
        rows = slice(side * ROWS, (side + 1) * ROWS)
        c, s = divmod(slab_index, SLABS)
        if c == 0:
            qbuf[b, s] = head_norm(slab, gain[0:1, :]).astype(BF16)
        elif c == 1:
            key = head_norm(slab, gain[1:2, :]).astype(BF16)
            first = jnp.broadcast_to(tk[b, 0:1, s * 128:(s + 1) * 128], key.shape)
            kbuf[b, s, rows, :] = jnp.where(usable, key, first)
        else:
            vbuf[b, s, rows, :128] = jnp.where(usable, slab, 0.0).astype(BF16)
            vbuf[b, s, rows, 128:] = onehot(usable)

    def project(side, b, slabs):
        for i in range(0, len(slabs), 2):
            pair = slabs[i:i + 2]
            out = dot(normed[2 * side + b], wqkv[:, pair[0] * 128:(pair[-1] + 1) * 128])
            for t, slab_index in enumerate(pair):
                put(side, b, slab_index, out[:, t * 128:(t + 1) * 128])

    embed(0)

    @pl.loop(0, 2)
    def _(half):
        norm(0, half, mod)

    embed(1)

    for b in range(2):
        norm(1, b, mod_mate)
        project(0, b, list(range(3 * SLABS)))

    for b in range(2):
        project(1, b, list(range(SLABS, 3 * SLABS)))

    def half_rows(b):
        return slice(b * HALF, (b + 1) * HALF) if isinstance(b, int) else pl.ds(
            pl.multiple_of(b * HALF, HALF), HALF
        )

    def exchange(b):
        return remote(
            normed.at[0, half_rows(b)], got.at[b], xsend.at[b], xrecv.at[b], sibling_id
        )

    def project_out(b, half, into):
        rows = att[b, pl.ds(pl.multiple_of(half * HALF, HALF), HALF), :]
        for start, size in CHUNKS:
            normed[into, half_rows(b), start:start + size] = dot(
                rows, wout[:, start:start + size]
            ).astype(BF16)

    lower = iota((ROWS, 128), 1) < HEAD
    wout_load.wait()
    wfin_load.wait()

    def attend(b):
        for s in range(SLABS):
            query, key, value = qbuf[b, s], kbuf[b, s], vbuf[b, s]
            parts = []
            for head in (lower, ~lower):
                scores = lax.dot_general(
                    jnp.where(head, query, jnp.zeros_like(query)), key, NT,
                    preferred_element_type=F32,
                )
                highest = jnp.max(scores, axis=-1, keepdims=True)
                raised = jnp.exp2((scores - highest) * (HEAD ** (-0.5) * LOG2E)).astype(BF16)
                both = dot(raised, value)
                parts.append(both[:, :128] / both[:, 128:])
            att[b, :, s * 128:(s + 1) * 128] = jnp.where(lower, parts[0], parts[1]).astype(BF16)

    @pl.loop(0, 2)
    def _(b):
        attend(b)
        project_out(b, other, 0)
        exchange(b).start()

    for b in range(2):
        project_out(b, core, 1)

    block = 96
    for b in range(2):
        exchange(b).wait_recv()
        gate, shift, scale = (mod[i, b:b + 1, :] for i in (2, 3, 4))

        @pl.loop(0, HALF // block)
        def _(i):
            rows = pl.ds(pl.multiple_of(i * block, block), block)
            kept = normed[1, pl.ds(pl.multiple_of(b * HALF + i * block, block), block), :]
            mixed = kept.astype(F32) + got[b, rows, :].astype(F32)
            mine = pl.ds(pl.multiple_of(core * HALF + i * block, block), block)
            state = hid[0, mine, :] + gate * mixed
            centred = state - jnp.mean(state, axis=-1, keepdims=True)
            spread = jnp.mean(centred * centred, axis=-1, keepdims=True)
            final = (centred * lax.rsqrt(spread + EPS) * (1.0 + scale) + shift).astype(BF16)
            normed[2, pl.ds(pl.multiple_of(b * HALF + i * block, block), block), :] = final

    velocity = lax.dot_general(normed[2], wfin[...], NT, preferred_element_type=F32)
    guided = velocity[HALF:] + GUIDE * (velocity[:HALF] - velocity[HALF:])
    row = iota((HALF, CH), 0)
    upper = jnp.where(row >= TILES, 1, 0)
    position = (row - upper * TILES) * TILE + 2 * core + upper
    change = jnp.where(position < own_len, STEP * guided, 0.0)
    change = jnp.concatenate([change[:TILES], change[TILES:]], axis=1).astype(BF16)
    home_b[...] = dot(unsettle, change).astype(BF16).reshape(XY, 16, 128)

    def return_b(k):
        return remote(
            home_b.at[plane_peer(k)], back_b.at[xy], hsend_b.at[k], hrecv_b.at[xy], plane_id(k)
        )

    def arrive_b(k):
        at = plane_peer(k)
        return remote(home_b.at[at], back_b.at[at], hsend_b.at[k], hrecv_b.at[at], plane_id(k))

    @pl.loop(1, XY)
    def _(k):
        return_b(k).start()

    back_b[xy] = home_b[xy]
    row, col = iota((256, 256), 0), iota((256, 256), 1)
    reorder = onehot(col == ((row >> 1) & 15) * 16 + (row & 1) * 8 + (row >> 5))
    collect = onehot(iota((TILES, 256), 1).astype(F32) == bucket_column)

    @pl.loop(1, XY)
    def _(k):
        arrive_b(k).wait_recv()

    home_a[...] = dot(reorder, back_b[...].reshape(256, 128)).astype(BF16).reshape(Z, 32, 128)

    def return_a(k):
        return remote(
            home_a.at[z_peer(k)], back_a.at[z], hsend_a.at[k], hrecv_a.at[z], z_id(k)
        )

    def arrive_a(k):
        at = z_peer(k)
        return remote(home_a.at[at], back_a.at[at], hsend_a.at[k], hrecv_a.at[at], z_id(k))

    @pl.loop(1, Z)
    def _(k):
        return_a(k).start()

    back_a[z] = home_a[z]

    @pl.loop(1, Z)
    def _(k):
        send_a(k).wait_send()

    @pl.loop(1, XY)
    def _(k):
        send_b(k).wait_send()
        return_b(k).wait_send()

    send_c.wait_send()
    mod_copy.wait_send()
    for b in range(2):
        exchange(b).wait_send()

    @pl.loop(1, Z)
    def _(k):
        arrive_a(k).wait_recv()

    out_ref[...] = lat[...] + dot(collect, back_a[...].reshape(256, 128))

    @pl.loop(1, Z)
    def _(k):
        return_a(k).wait_send()


def step(*operands):
    hbm = pl.BlockSpec(memory_space=pltpu.HBM)
    smem = pl.BlockSpec(memory_space=pltpu.SMEM)
    narrow, wide = pltpu.VMEM((Z, 32, 128), BF16), pltpu.VMEM((XY, 16, 128), BF16)
    dma = pltpu.SemaphoreType.DMA
    return pl.pallas_call(
        step_kernel,
        out_shape=jax.ShapeDtypeStruct((TILES, 128), F32),
        in_specs=[hbm] * 10 + [smem] * 2,
        out_specs=pl.BlockSpec(memory_space=pltpu.VMEM),
        scratch_shapes=[
            pltpu.VMEM((TILES, 128), F32),
            pltpu.VMEM((TILES, 128), jnp.int32),
            pltpu.VMEM((Z * XY, TILES), jnp.int32),
            pltpu.VMEM((5, 2, D), F32),
            pltpu.VMEM((2, 2, D), F32),
            pltpu.VMEM((3, HEAD), F32),
            pltpu.VMEM((3, 128), F32),
            pltpu.VMEM((TEXT_PAD, 2, D), BF16),
            pltpu.VMEM((D, 2, WIDTH), BF16),
            pltpu.VMEM((2, D, WIDTH), BF16),
            pltpu.VMEM((CH, D), BF16),
            pltpu.VMEM((D, 3 * WIDTH), BF16),
            pltpu.VMEM((WIDTH, D), BF16),
            pltpu.VMEM((CH, D), BF16),
            pltpu.VMEM((2, TEXT_PAD, WIDTH), BF16),
            pltpu.VMEM((2, TEXT_PAD, WIDTH), BF16),
            pltpu.VMEM((2, 2, TILES, 128), BF16),
            pltpu.VMEM((4, ROWS, D), BF16),
            pltpu.VMEM((2, SLABS, ROWS, 128), BF16),
            pltpu.VMEM((2, SLABS, KEYS, 128), BF16),
            pltpu.VMEM((2, SLABS, KEYS, 256), BF16),
            pltpu.VMEM((2, ROWS, WIDTH), BF16),
            pltpu.VMEM((2, HALF, D), BF16),
            pltpu.VMEM((2, ROWS, D), F32),
            pltpu.VMEM((2, ROWS, CH), BF16),
            pltpu.VMEM((XY, 2, 16, TILES), F32),
            narrow, narrow, narrow, pltpu.VMEM((XY, 32, 128), BF16), wide, wide, narrow, narrow,
            dma((12,)), dma((2,)), dma((Z,)), dma((Z,)), dma((XY,)), dma((XY,)),
            dma, dma, dma((2,)), dma((2,)),
            dma((XY,)), dma((XY,)), dma((Z,)), dma((Z,)),
        ],
        compiler_params=pltpu.CompilerParams(
            collective_id=0, has_side_effects=True, vmem_limit_bytes=63 << 20
        ),
        name="step",
    )(*operands)


def shards(
    latents, tile_slot, live, partner, text_states, modulation,
    w_embed, w_qkv, w_text_kv, w_out, w_final, norm_gains,
):
    return step(
        latents, tile_slot.reshape(TILES, 128), modulation[0].transpose(1, 0, 2),
        norm_gains, text_states[0].transpose(1, 0, 2),
        w_text_kv, w_embed, w_qkv.transpose(1, 0, 2), w_out, w_final.T, live, partner,
    )


def solution(mesh):
    placed = (
        P("groups", "mp"), P(), P(), P(),
        P("groups", None, None, None), P("groups", None, None, None),
        P(), P(None, None, "mp"), P(None, None, "mp"), P("mp", None), P(), P(),
    )
    return jax.shard_map(
        shards, mesh=mesh, in_specs=placed, out_specs=P("groups", "mp"), check_vma=False
    )
```
